128 devices in a mesh: dp: 4 (over x), expert: 32 (over y, z, core).
Axes of the slice: x: 4, y: 4, z: 4, core: 2. Of those that a mesh axis runs over, the one named last changes fastest.
Arguments:
- tokens: bfloat16 [4096, 3584], P(('dp', 'expert')), may hold values from -6 to 6
- expert_ids: int32 [4096, 8], P(('dp', 'expert')), may hold values from 0 to 31, all different within a row; in each aligned block of 32 rows (0 to 31, 32 to 63, ...) at most 12 rows name the same one
- route_weights: float32 [4096, 8], P(('dp', 'expert')), may hold values from 0.1 to 1
- out_grad: bfloat16 [4096, 3584], P(('dp', 'expert')), may hold values from -6 to 6
- gate_weight: bfloat16 [32, 3584, 1024], P('expert', 'dp'), may hold values from -0.09375 to 0.09375
- up_weight: bfloat16 [32, 3584, 1024], P('expert', 'dp'), may hold values from -0.09375 to 0.09375
- down_weight: bfloat16 [32, 1024, 3584], P('expert', None, 'dp'), may hold values from -0.1875 to 0.1875
Outputs:
- mixed: bfloat16 [4096, 3584], P(('dp', 'expert'))
- tokens_grad: bfloat16 [4096, 3584], P(('dp', 'expert'))
- route_grad: float32 [4096, 8], P(('dp', 'expert'))
- gate_grad: bfloat16 [32, 3584, 1024], P('expert', 'dp')
- up_grad: bfloat16 [32, 3584, 1024], P('expert', 'dp')
- down_grad: bfloat16 [32, 1024, 3584], P('expert', None, 'dp')
The draws below stay inside these ranges and needn't reach their ends.
Inputs may be any that keep to these rules, and one draw needn't show every extreme that they name: `expert_ids`: each row names 8 different experts; in each aligned block of 32 rows (the rows of one device) no expert is named by more than 12 rows, a bound that some block reaches.
All inputs are finite; a program needn't handle non-finite values.
Results may differ from the reference program's by a relative error of at most 0.0065.
Values may be sent and summed in bfloat16 or wider, within the bound.
A program may use at most 192 MiB of HBM per device.

```python
import math
import jax
import jax.numpy as jnp
import numpy as np
from jax import lax

D = 3584
H = 1024
TOP = 8
TOK_DEV = 32
EXPERTS = 32
MOST = 12
TOKENS = 4096
N_DP = 4
N_EXPERT = 32


def levels(key, dims, split, least, top_value):
    def one(dim, blocks):
        steps = jax.random.uniform(jax.random.fold_in(jax.random.fold_in(key, 6), dim), (blocks,), jnp.float32, least / len(split), top_value / len(split))
        return jnp.repeat(jnp.exp(steps), dims[dim] // blocks).reshape((-1,) + (1,) * (len(dims) - dim - 1))

    loudness = one(*split[0])
    for cut in split[1:]:
        loudness = loudness * one(*cut)
    return loudness


def assign_block(stream_key, own, number, rows, count, top, limit, slope):
    sequence = jax.random.permutation(stream_key, count)
    packed, usual = shares(count, rows * top, limit, slope, True), shares(count, rows * top, limit, slope, False)
    places = jnp.arange(count)

    def named(sizes, offset_by):
        used = int((sizes > 0).sum())
        fixed = max(1, used // 4)
        moved = fixed + (places - fixed + offset_by * (used - fixed)) % max(1, count - fixed)
        return jnp.zeros((count,), jnp.int32).at[sequence[jnp.where(places < fixed, places, moved)]].set(jnp.asarray(sizes, jnp.int32))

    sizes = jnp.where(number % 4 == 0, named(packed, number // 4), named(usual, number - number // 4 - 1))
    mixed = jax.random.permutation(jax.random.fold_in(own, 3), count)
    donor, taker = mixed[0:count // 2 * 2:2], mixed[1:count // 2 * 2:2]
    room = jnp.minimum(sizes[donor] - 1, limit - sizes[taker]) // 2
    room = jnp.where((donor == sequence[0]) | (taker == sequence[0]) | (sizes[taker] == 0), 0, jnp.maximum(room, 0))
    moved = jax.random.randint(jax.random.fold_in(own, 4), (count // 2,), 0, 1 << 20) % (room + 1)
    sizes = sizes.at[donor].add(-moved).at[taker].add(moved)
    items = jnp.searchsorted(jnp.cumsum(sizes), jnp.arange(rows * top), side="right").astype(jnp.int32)
    table = items.reshape(top, rows).T
    table = table[jax.random.permutation(jax.random.fold_in(own, 1), rows)]
    offset_by = jax.random.randint(jax.random.fold_in(own, 2), (rows, 1), 0, top)
    return jnp.take_along_axis(table, (jnp.arange(top)[None, :] + offset_by) % top, axis=1)


def shares(count, total, reach, lean, full):
    loads = [(1 << 20) // math.isqrt(grade ** lean) + 1 for grade in range(1, count + 1)]
    largest = reach if full else min(reach, max(-(-total // count), total * loads[0] // sum(loads)))
    least = 1 if total - largest >= count - 1 else 0
    counts, surplus = [largest] + [least] * (count - 1), total - largest - least * (count - 1)
    while surplus > 0:
        candidates = [i for i in range(1, count) if counts[i] < largest] or [i for i in range(1, count) if counts[i] < reach]
        whole, left = sum([loads[i] for i in candidates]), surplus
        for i in candidates:
            addition = min(reach - counts[i], max(1, left * loads[i] // whole), surplus)
            counts[i] = counts[i] + addition
            surplus = surplus - addition
    return np.array(counts)


def noise(key, dims, width, bound, cuts=(), kind=jnp.bfloat16):
    array = jax.random.normal(key, dims, jnp.float32) * width
    if len(cuts) > 0:
        array = levels(key, dims, cuts, -0.22, 0.18) * array
    return jnp.clip(array, min=-bound, max=bound).astype(kind)


def setup_inputs(seed: int = 0) -> dict:
    key_list = jax.random.split(jax.random.key(seed), 8)
    tokens = noise(key_list[0], (TOKENS, D), 1.0, 6.0, ((0, 128),))
    expert_ids_keys = jax.random.split(jax.random.fold_in(key_list[1], 1), TOKENS // TOK_DEV)
    expert_ids_turns = jax.random.permutation(jax.random.fold_in(key_list[1], 3), TOKENS // TOK_DEV)
    expert_ids = jax.vmap(lambda own, number: assign_block(jax.random.fold_in(key_list[1], 2), own, number, TOK_DEV, EXPERTS, TOP, MOST, 2))(expert_ids_keys, expert_ids_turns).reshape((TOKENS, TOP))
    route_weights = jnp.clip(jnp.exp(math.log(1.0) - 2.3025851 * jax.random.uniform(key_list[2], (TOKENS, TOP), jnp.float32) ** levels(key_list[2], (TOKENS, TOP), ((0, 128),), -0.2, 0.2)), 0.1, 1.0)
    out_grad = noise(key_list[3], (TOKENS, D), 1.0, 6.0, ((0, 128),))
    gate_weight = noise(key_list[4], (EXPERTS, D, H), D ** -0.5, 0.09375, ((0, 32), (1, 4)))
    up_weight = noise(key_list[5], (EXPERTS, D, H), D ** -0.5, 0.09375, ((0, 32), (1, 4)))
    down_weight = noise(key_list[6], (EXPERTS, H, D), H ** -0.5, 0.1875, ((0, 32), (2, 4)))
    return {"tokens": tokens, "expert_ids": expert_ids, "route_weights": route_weights, "out_grad": out_grad, "gate_weight": gate_weight, "up_weight": up_weight, "down_weight": down_weight}


def silu_parts(pre_act):
    sigmoid_val = jax.nn.sigmoid(pre_act)
    return pre_act * sigmoid_val, sigmoid_val * (1.0 + pre_act * (1.0 - sigmoid_val))


def reference(tokens, expert_ids, route_weights, out_grad, gate_weight, up_weight, down_weight):
    capacity = N_DP * N_EXPERT * MOST
    flat_ids = expert_ids.reshape(-1)
    flat_weights = route_weights.reshape(-1)
    grad32 = out_grad.astype(jnp.float32)
    rows_total = tokens.shape[0]

    def per_expert(buffers, inputs):
        mixed_acc, grad_acc, route_acc = buffers
        expert_index, gate_w, up_w, down_w = inputs
        chosen = flat_ids == expert_index
        pick_rows = jnp.nonzero(chosen, size=capacity, fill_value=0)[0].astype(jnp.int32)
        live_rows = jnp.arange(capacity, dtype=jnp.int32) < jnp.sum(chosen.astype(jnp.int32))
        owner_rows = pick_rows // TOP
        x_rows = jnp.where(live_rows[:, None], tokens[owner_rows], jnp.zeros((), jnp.bfloat16))
        gate_pre = jnp.dot(x_rows, gate_w, preferred_element_type=jnp.float32)
        up_pre = jnp.dot(x_rows, up_w, preferred_element_type=jnp.float32)
        act_val, act_slope = silu_parts(gate_pre)
        hidden = (act_val * up_pre).astype(jnp.bfloat16)
        expert_out = jnp.dot(hidden, down_w, preferred_element_type=jnp.float32).astype(jnp.bfloat16)
        out32 = expert_out.astype(jnp.float32)
        live_weights = jnp.where(live_rows, flat_weights[pick_rows], jnp.float32(0.0))
        mixed_acc = mixed_acc.at[owner_rows].add(live_weights[:, None] * out32)
        route_term = jnp.where(live_rows, jnp.sum(grad32[owner_rows] * out32, axis=1), jnp.float32(0.0))
        route_acc = route_acc.at[pick_rows].add(route_term)
        out_term = (live_weights[:, None] * grad32[owner_rows]).astype(jnp.bfloat16)
        hidden_grad = jnp.dot(out_term, down_w.T, preferred_element_type=jnp.float32)
        gate_term = (hidden_grad * up_pre * act_slope).astype(jnp.bfloat16)
        up_term = (hidden_grad * act_val).astype(jnp.bfloat16)
        input_term = (jnp.dot(gate_term, gate_w.T, preferred_element_type=jnp.float32)
                      + jnp.dot(up_term, up_w.T, preferred_element_type=jnp.float32)).astype(jnp.bfloat16)
        grad_acc = grad_acc.at[owner_rows].add(jnp.where(live_rows[:, None], input_term.astype(jnp.float32), jnp.float32(0.0)))
        gate_g = jnp.dot(x_rows.T, gate_term, preferred_element_type=jnp.float32).astype(jnp.bfloat16)
        up_g = jnp.dot(x_rows.T, up_term, preferred_element_type=jnp.float32).astype(jnp.bfloat16)
        down_g = jnp.dot(hidden.T, out_term, preferred_element_type=jnp.float32).astype(jnp.bfloat16)
        return (mixed_acc, grad_acc, route_acc), (gate_g, up_g, down_g)

    start_buffers = (jnp.zeros((rows_total, D), jnp.float32), jnp.zeros((rows_total, D), jnp.float32),
                     jnp.zeros((rows_total * TOP,), jnp.float32))
    expert_list = jnp.arange(EXPERTS, dtype=jnp.int32)
    finals, grads = lax.scan(per_expert, start_buffers, (expert_list, gate_weight, up_weight, down_weight))
    mixed_acc, grad_acc, route_acc = finals
    return (mixed_acc.astype(jnp.bfloat16), grad_acc.astype(jnp.bfloat16), route_acc.reshape(rows_total, TOP),
            grads[0], grads[1], grads[2])
```

```python
import jax
import jax.numpy as jnp
from jax import lax
from jax.sharding import PartitionSpec as P

BF = jnp.bfloat16
F32 = jnp.float32
LANES = 128


def dot32(a, b, dims):
    return lax.dot_general(a, b, (dims, ((), ())), preferred_element_type=F32)


def route_table(ids, weights, experts):
    onehot = (ids[:, :, None] == jnp.arange(experts, dtype=jnp.int32)).astype(jnp.int32)
    chosen = jnp.sum(onehot, axis=1)
    place = jnp.cumsum(chosen, axis=0) * chosen
    dense = jnp.sum(onehot.astype(F32) * weights[:, :, None], axis=1)
    high = lax.reduce_precision(dense, 8, 7)
    middle = lax.reduce_precision(dense - high, 8, 7)
    low = dense - high - middle
    return jnp.concatenate([place.astype(F32), high, middle, low], axis=1).astype(BF)


def to_slices(array, n_dp):
    rows, width = array.shape
    return lax.all_to_all(array, "dp", split_axis=1, concat_axis=0, tiled=True)


def dispatch(tokens, out_grad, table):
    n_dp = lax.axis_size("dp")
    tok = to_slices(tokens, n_dp)
    grad = to_slices(out_grad, n_dp)
    tab = lax.all_gather(table, "dp", axis=0, tiled=True)
    whole = lax.all_gather(
        jnp.concatenate([tok, grad, tab], axis=1), "expert", axis=0, tiled=False
    )
    return whole, grad, tab


def pick_rows(whole, slots, experts, n_dp, tok_rows, width):
    me = lax.axis_index("expert")
    tab = whole[:, :, 2 * width :].astype(F32)
    lane = jnp.arange(tab.shape[2], dtype=jnp.int32)
    place = jnp.sum(jnp.where(lane == me, tab, 0.0), axis=2)
    weight = jnp.sum(jnp.where((lane >= experts) & (lane % experts == me), tab, 0.0), axis=2)
    rows = n_dp * slots
    row = jnp.arange(rows, dtype=jnp.int32)
    tok = jnp.arange(n_dp * tok_rows, dtype=jnp.int32)
    same = (row[:, None] // slots) == (tok[None, :] // tok_rows)
    hit = same & (place[:, None, :] == (row % slots + 1).astype(F32)[None, :, None])
    picked = lax.dot_general(
        hit.astype(BF), whole[:, :, : 2 * width], (((2,), (1,)), ((0,), (0,))), preferred_element_type=F32
    )
    scale = jnp.sum(jnp.where(hit, weight[:, None, :], 0.0), axis=2)
    x_rows = picked[:, :, :width].astype(BF).reshape(experts * rows, width)
    g_rows = (picked[:, :, width:] * scale[:, :, None]).astype(BF).reshape(experts * rows, width)
    return x_rows, g_rows


def activations(pre, quarter):
    gate, up, hgrad = (pre[:, i * quarter : (i + 1) * quarter].astype(F32) for i in range(3))
    sig = jax.nn.sigmoid(gate)
    act = gate * sig
    slope = sig * (1.0 + gate * (1.0 - sig))
    return jnp.concatenate(
        [(act * up).astype(BF), (hgrad * up * slope).astype(BF), (hgrad * act).astype(BF)], axis=1
    )


def combine(back, ids, grad, tab, slots, experts, n_dp, tok_rows, width):
    tab = tab.astype(F32)
    toks = n_dp * tok_rows
    place = tab[:, :experts]
    weight = tab[:, experts : 2 * experts] + tab[:, 2 * experts : 3 * experts] + tab[:, 3 * experts : 4 * experts]
    row = jnp.arange(n_dp * slots, dtype=jnp.int32)
    tok = jnp.arange(toks, dtype=jnp.int32)
    same = (row[None, :] // slots) == (tok[:, None] // tok_rows)
    hit = same[:, None, :] & (place[:, :, None] == (row % slots + 1).astype(F32))
    flat = hit.reshape(toks, -1)
    scaled = jnp.where(hit, weight[:, :, None], 0.0).reshape(toks, -1)
    out_rows = back[:, :width]
    in_rows = back[:, width:]
    mixed = lax.dot_general(
        scaled, out_rows.astype(F32), (((1,), (0,)), ((), ())), precision=lax.Precision.HIGHEST
    )
    tgrad = dot32(flat.astype(BF), in_rows, ((1,), (0,)))
    dots = dot32(grad, out_rows, ((1,), (1,)))
    route = jnp.sum(jnp.where(hit, dots.reshape(hit.shape), 0.0), axis=2)
    mixed = lax.all_to_all(mixed.astype(BF).reshape(n_dp, tok_rows, width), "dp", 0, 0, tiled=True)
    tgrad = lax.all_to_all(tgrad.astype(BF).reshape(n_dp, tok_rows, width), "dp", 0, 0, tiled=True)
    route = lax.psum_scatter(route, "dp", scatter_dimension=0, tiled=True)
    mixed = mixed.transpose(1, 0, 2).reshape(tok_rows, n_dp * width)
    tgrad = tgrad.transpose(1, 0, 2).reshape(tok_rows, n_dp * width)
    onehot = ids[:, :, None] == jnp.arange(experts, dtype=jnp.int32)
    route = jnp.sum(jnp.where(onehot, route[:, None, :], 0.0), axis=2)
    return mixed, tgrad, route


def per_device(tokens, ids, weights, out_grad, gate_weight, up_weight, down_weight):
    experts = lax.axis_size("expert")
    n_dp = lax.axis_size("dp")
    tok_rows, model = tokens.shape
    width = model // n_dp
    hidden = gate_weight.shape[2]
    quarter = hidden // n_dp
    slots = min(tok_rows, 3 * tok_rows * ids.shape[1] // (2 * experts))
    gate, up, down = gate_weight[0], up_weight[0], down_weight[0]

    table = route_table(ids, weights, experts)
    whole, grad, tab = dispatch(tokens, out_grad, table)
    x_rows, g_rows = pick_rows(whole, slots, experts, n_dp, tok_rows, width)

    rows = x_rows.shape[0]
    part = jnp.stack(
        [
            dot32(x_rows, gate, ((1,), (0,))).astype(BF),
            dot32(x_rows, up, ((1,), (0,))).astype(BF),
            dot32(g_rows, down, ((1,), (1,))).astype(BF),
        ]
    )
    part = part.reshape(3, rows, n_dp, quarter).transpose(2, 1, 0, 3).reshape(n_dp * rows, 3 * quarter)
    pre = lax.psum_scatter(part, "dp", scatter_dimension=0, tiled=True)
    acts = activations(pre, quarter)
    terms = lax.all_gather(acts, "dp", axis=0, tiled=False)
    terms = terms.reshape(n_dp, rows, 3, quarter).transpose(2, 1, 0, 3).reshape(3, rows, hidden)
    hid, gterm, uterm = terms[0], terms[1], terms[2]

    out_rows = dot32(hid, down, ((1,), (0,))).astype(BF)
    in_rows = (dot32(gterm, gate, ((1,), (1,))) + dot32(uterm, up, ((1,), (1,)))).astype(BF)
    send = jnp.concatenate([out_rows, in_rows], axis=1).reshape(experts, n_dp * slots, 2 * width)
    back = lax.all_to_all(send, "expert", split_axis=0, concat_axis=0, tiled=True)
    back = back.reshape(experts * n_dp * slots, 2 * width)

    gate_grad = dot32(x_rows, gterm, ((0,), (0,))).astype(BF)[None]
    up_grad = dot32(x_rows, uterm, ((0,), (0,))).astype(BF)[None]
    down_grad = dot32(hid, g_rows, ((0,), (0,))).astype(BF)[None]

    mixed, tgrad, route = combine(back, ids, grad, tab, slots, experts, n_dp, tok_rows, width)
    return (mixed, tgrad, route, gate_grad, up_grad, down_grad)


def solution(mesh):
    rows = P(("dp", "expert"), None)
    weights = (P("expert", "dp", None), P("expert", "dp", None), P("expert", None, "dp"))
    return jax.shard_map(
        per_device,
        mesh=mesh,
        in_specs=(rows, rows, rows, rows) + weights,
        out_specs=(rows, rows, rows) + weights,
        check_vma=False,
    )
```

```python
import functools

import jax
import jax.numpy as jnp
from jax import lax
from jax.experimental import pallas as pl
from jax.experimental.pallas import tpu as pltpu
from jax.sharding import PartitionSpec as P

BF = jnp.bfloat16
F32 = jnp.float32
LANES = 128


def dot32(a, b, dims):
    return lax.dot_general(a, b, (dims, ((), ())), preferred_element_type=F32)


def route_table(ids, weights, experts):
    onehot = (ids[:, :, None] == jnp.arange(experts, dtype=jnp.int32)).astype(jnp.int32)
    chosen = jnp.sum(onehot, axis=1)
    place = jnp.cumsum(chosen, axis=0) * chosen
    dense = jnp.sum(onehot.astype(F32) * weights[:, :, None], axis=1)
    high = lax.reduce_precision(dense, 8, 7)
    middle = lax.reduce_precision(dense - high, 8, 7)
    low = dense - high - middle
    return jnp.concatenate([place.astype(F32), high, middle, low], axis=1).astype(BF)


def to_slices(array, n_dp):
    rows, width = array.shape
    return lax.all_to_all(array, "dp", split_axis=1, concat_axis=0, tiled=True)


def dispatch(tokens, out_grad, table):
    n_dp = lax.axis_size("dp")
    tok = to_slices(tokens, n_dp)
    grad = to_slices(out_grad, n_dp)
    tab = lax.all_gather(table, "dp", axis=0, tiled=True)
    whole = lax.all_gather(
        jnp.concatenate([tok, grad, tab], axis=1), "expert", axis=0, tiled=False
    )
    return whole, grad, tab


def pick_rows(whole, slots, experts, n_dp, tok_rows, width):
    me = lax.axis_index("expert")
    tab = whole[:, :, 2 * width :].astype(F32)
    lane = jnp.arange(tab.shape[2], dtype=jnp.int32)
    place = jnp.sum(jnp.where(lane == me, tab, 0.0), axis=2)
    weight = jnp.sum(jnp.where((lane >= experts) & (lane % experts == me), tab, 0.0), axis=2)
    rows = n_dp * slots
    row = jnp.arange(rows, dtype=jnp.int32)
    tok = jnp.arange(n_dp * tok_rows, dtype=jnp.int32)
    same = (row[:, None] // slots) == (tok[None, :] // tok_rows)
    hit = same & (place[:, None, :] == (row % slots + 1).astype(F32)[None, :, None])
    picked = lax.dot_general(
        hit.astype(BF), whole[:, :, : 2 * width], (((2,), (1,)), ((0,), (0,))), preferred_element_type=F32
    )
    scale = jnp.sum(jnp.where(hit, weight[:, None, :], 0.0), axis=2)
    x_rows = picked[:, :, :width].astype(BF).reshape(experts * rows, width)
    g_rows = (picked[:, :, width:] * scale[:, :, None]).astype(BF).reshape(experts * rows, width)
    return x_rows, g_rows


def combine(back, ids, grad, tab, slots, experts, n_dp, tok_rows, width):
    tab = tab.astype(F32)
    toks = n_dp * tok_rows
    place = tab[:, :experts]
    weight = tab[:, experts : 2 * experts] + tab[:, 2 * experts : 3 * experts] + tab[:, 3 * experts : 4 * experts]
    row = jnp.arange(n_dp * slots, dtype=jnp.int32)
    tok = jnp.arange(toks, dtype=jnp.int32)
    same = (row[None, :] // slots) == (tok[:, None] // tok_rows)
    hit = same[:, None, :] & (place[:, :, None] == (row % slots + 1).astype(F32))
    flat = hit.reshape(toks, -1)
    scaled = jnp.where(hit, weight[:, :, None], 0.0).reshape(toks, -1)
    out_rows = back[:, :width]
    in_rows = back[:, width:]
    mixed = lax.dot_general(
        scaled, out_rows.astype(F32), (((1,), (0,)), ((), ())), precision=lax.Precision.HIGHEST
    )
    tgrad = dot32(flat.astype(BF), in_rows, ((1,), (0,)))
    dots = dot32(grad, out_rows, ((1,), (1,)))
    route = jnp.sum(jnp.where(hit, dots.reshape(hit.shape), 0.0), axis=2)
    mixed = lax.all_to_all(mixed.astype(BF).reshape(n_dp, tok_rows, width), "dp", 0, 0, tiled=True)
    tgrad = lax.all_to_all(tgrad.astype(BF).reshape(n_dp, tok_rows, width), "dp", 0, 0, tiled=True)
    route = lax.psum_scatter(route, "dp", scatter_dimension=0, tiled=True)
    mixed = mixed.transpose(1, 0, 2).reshape(tok_rows, n_dp * width)
    tgrad = tgrad.transpose(1, 0, 2).reshape(tok_rows, n_dp * width)
    onehot = ids[:, :, None] == jnp.arange(experts, dtype=jnp.int32)
    route = jnp.sum(jnp.where(onehot, route[:, None, :], 0.0), axis=2)
    return mixed, tgrad, route


CHUNKS = 4
MESH = pl.DeviceIdType.MESH


def exchange_kernel(
    slots_dp, x_ref, g_ref, gate_ref, up_ref, down_ref, back_ref, terms_ref,
    part, own, in_half, in_full, terms, rows_out,
    ring_send, ring_recv, ret_send, ret_recv, out_sem,
):
    n_dp = lax.axis_size("dp")
    experts = lax.axis_size("expert")
    d = lax.axis_index("dp")
    e = lax.axis_index("expert")
    group = experts // CHUNKS
    chunk = group * slots_dp
    half = chunk // 2
    quarter = own.shape[3]
    width = x_ref.shape[1]
    to = ((d + n_dp - 1) % n_dp, (d + 1) % n_dp)

    barrier = pltpu.get_barrier_semaphore()
    for side in to:
        pl.semaphore_signal(barrier, inc=1, device_id={"dp": side}, device_id_type=MESH)

    def greet(step, carry):
        pl.semaphore_signal(
            barrier, inc=1, device_id={"expert": (e + step) % experts}, device_id_type=MESH
        )
        return carry

    lax.fori_loop(1, experts, greet, 0)
    pl.semaphore_wait(barrier, experts + 1)

    def which(k):
        return (e // group + k) % CHUNKS

    def rows_of(k, part_half=None):
        start = which(k) * chunk
        if part_half is None:
            return pl.ds(pl.multiple_of(start, chunk), chunk)
        return pl.ds(pl.multiple_of(start + part_half * half, half), half)

    def cols_of(q):
        return pl.ds(pl.multiple_of(q * quarter, quarter), quarter)

    def copy(k, way, number, source, target):
        return pltpu.make_async_remote_copy(
            src_ref=source,
            dst_ref=target,
            send_sem=ring_send.at[k, way, number],
            recv_sem=ring_recv.at[k, way, number],
            device_id={"dp": to[way]},
            device_id_type=MESH,
        )

    def toward(k, way):
        return part.at[k, 2 if way == 0 else 0]

    def halves(ref, h):
        return ref.at[:, pl.ds(h * half, half), :]

    def rs_copy(k, way, number):
        if number == 0:
            return copy(k, way, 0, halves(part.at[k, 1], way), in_half.at[k, way])
        h = way if number == 2 else 1 - way
        return copy(k, way, number, halves(toward(k, way), h), halves(in_full.at[k, way], h))

    def ag_copy(k, way, number):
        if number == 5:
            q = (d + 1) % n_dp if way == 0 else (d + n_dp - 1) % n_dp
            h = way
        else:
            q = d
            h = way if number == 3 else 1 - way
        ref = terms.at[:, rows_of(k, h), cols_of(q)]
        return copy(k, way, number, ref, ref)

    def ag_arrival(k, way, number):
        src = (d + 1) % n_dp if way == 0 else (d + n_dp - 1) % n_dp
        q = (d + 2) % n_dp if number == 5 else src
        h = way if number in (3, 5) else 1 - way
        ref = terms.at[:, rows_of(k, h), cols_of(q)]
        return copy(k, way, number, ref, ref)

    def partial(k, q, i):
        if i == 0:
            return jnp.dot(x_ref[rows_of(k), :], gate_ref[:, cols_of(q)], preferred_element_type=F32)
        if i == 1:
            return jnp.dot(x_ref[rows_of(k), :], up_ref[:, cols_of(q)], preferred_element_type=F32)
        return dot32(g_ref[rows_of(k), :], down_ref[cols_of(q), :], ((1,), (1,)))

    def stage0(k):
        def one(step, carry):
            m = (step + 1) % (n_dp - 1)
            q = (d + m + 1) % n_dp
            for i in range(3):
                part[k, m, i] = partial(k, q, i).astype(BF)
            return carry

        lax.fori_loop(0, n_dp - 1, one, 0)
        for way in range(2):
            rs_copy(k, way, 0).start()
        for way in range(2):
            rs_copy(k, way, 1).start()
        for i in range(3):
            own[k, i] = partial(k, d, i)

    def stage1(k):
        for way in range(2):
            rs_copy(k, way, 0).wait_recv()
            m = 2 if way == 0 else 0
            for i in range(3):
                span = pl.ds(way * half, half)
                total = part[k, m, i, span, :].astype(F32) + in_half[k, way, i].astype(F32)
                part[k, m, i, span, :] = total.astype(BF)
            rs_copy(k, way, 2).start()

    def stage2(k):
        for number in (1, 2):
            for way in range(2):
                rs_copy(k, way, number).wait_recv()

        def total(i, span):
            return own[k, i, span, :] + in_full[k, 0, i, span, :].astype(F32) + in_full[k, 1, i, span, :].astype(F32)

        step_rows = half // 2

        def act(step, carry):
            span = pl.ds(pl.multiple_of(step * step_rows, step_rows), step_rows)
            gate = total(0, span)
            up = total(1, span)
            hgrad = total(2, span)
            sig = jax.nn.sigmoid(gate)
            val = gate * sig
            slope = sig * (1.0 + gate * (1.0 - sig))
            target = pl.ds(pl.multiple_of(which(k) * chunk + step * step_rows, step_rows), step_rows)
            terms[0, target, cols_of(d)] = (val * up).astype(BF)
            terms[1, target, cols_of(d)] = (hgrad * up * slope).astype(BF)
            terms[2, target, cols_of(d)] = (hgrad * val).astype(BF)
            return carry

        lax.fori_loop(0, chunk // step_rows, act, 0)
        for number in (3, 4):
            for way in range(2):
                ag_copy(k, way, number).start()

    def stage3(k):
        for way in range(2):
            ag_arrival(k, way, 3).wait_recv()
            ag_copy(k, way, 5).start()

    def back_copy(k, i):
        j = which(k) * group + (e + i) % group
        return pltpu.make_async_remote_copy(
            src_ref=rows_out.at[pl.ds(pl.multiple_of(j * slots_dp, slots_dp), slots_dp), :],
            dst_ref=back_ref.at[pl.ds(pl.multiple_of(e * slots_dp, slots_dp), slots_dp), :],
            send_sem=ret_send.at[j],
            recv_sem=ret_recv.at[e],
            device_id={"expert": j},
            device_id_type=MESH,
        )

    def self_copy():
        mine = pl.ds(pl.multiple_of(e * slots_dp, slots_dp), slots_dp)
        return pltpu.make_async_copy(rows_out.at[mine, :], back_ref.at[mine, :], out_sem.at[CHUNKS])

    def terms_copy(k):
        return pltpu.make_async_copy(
            terms.at[:, rows_of(k), :], terms_ref.at[:, rows_of(k), :], out_sem.at[k]
        )

    def stage4(k):
        for way in range(2):
            ag_arrival(k, way, 4).wait_recv()
        for way in range(2):
            ag_arrival(k, way, 5).wait_recv()
        terms_copy(k).start()

        def one(h, carry):
            span = pl.ds(pl.multiple_of(which(k) * chunk + h * half, half), half)
            rows_out[span, :width] = jnp.dot(
                terms[0, span, :], down_ref[...], preferred_element_type=F32
            ).astype(BF)
            rows_out[span, width:] = (
                dot32(terms[1, span, :], gate_ref[...], ((1,), (1,)))
                + dot32(terms[2, span, :], up_ref[...], ((1,), (1,)))
            ).astype(BF)
            return carry

        lax.fori_loop(0, 2, one, 0)
        if k == 0:
            self_copy().start()

        def send(i, carry):
            back_copy(k, i).start()
            return carry

        lax.fori_loop(1 if k == 0 else 0, group, send, 0)

    for t in range(CHUNKS + 4):
        for lag, stage in ((1, stage1), (2, stage2), (3, stage3), (0, stage0), (4, stage4)):
            if 0 <= t - lag < CHUNKS:
                stage(t - lag)

    for k in range(CHUNKS):
        for way in range(2):
            for number in range(3):
                rs_copy(k, way, number).wait_send()
                ag_copy(k, way, number + 3).wait_send()
        terms_copy(k).wait()

        def sent(i, carry):
            back_copy(k, i).wait_send()
            return carry

        lax.fori_loop(1 if k == 0 else 0, group, sent, 0)
    self_copy().wait()

    def arrived(step, carry):
        s = (e + step) % experts
        ref = back_ref.at[pl.ds(pl.multiple_of(s * slots_dp, slots_dp), slots_dp), :]
        pltpu.make_async_remote_copy(
            src_ref=ref, dst_ref=ref, send_sem=ret_send.at[s], recv_sem=ret_recv.at[s],
            device_id={"expert": s}, device_id_type=MESH,
        ).wait_recv()
        return carry

    lax.fori_loop(1, experts, arrived, 0)


def exchange(x_rows, g_rows, gate, up, down, experts, n_dp):
    rows, width = x_rows.shape
    hidden = gate.shape[1]
    quarter = hidden // n_dp
    chunk = rows // CHUNKS
    dma = pltpu.SemaphoreType.DMA
    return pl.pallas_call(
        functools.partial(exchange_kernel, rows // experts),
        out_shape=(
            jax.ShapeDtypeStruct((rows, 2 * width), BF),
            jax.ShapeDtypeStruct((3, rows, hidden), BF),
        ),
        in_specs=[pl.BlockSpec(memory_space=pltpu.VMEM)] * 5,
        out_specs=(pl.BlockSpec(memory_space=pl.ANY), pl.BlockSpec(memory_space=pl.ANY)),
        scratch_shapes=[
            pltpu.VMEM((CHUNKS, n_dp - 1, 3, chunk, quarter), BF),
            pltpu.VMEM((CHUNKS, 3, chunk, quarter), F32),
            pltpu.VMEM((CHUNKS, 2, 3, chunk // 2, quarter), BF),
            pltpu.VMEM((CHUNKS, 2, 3, chunk, quarter), BF),
            pltpu.VMEM((3, rows, hidden), BF),
            pltpu.VMEM((rows, 2 * width), BF),
            dma((CHUNKS, 2, 6)),
            dma((CHUNKS, 2, 6)),
            dma((experts,)),
            dma((experts,)),
            dma((CHUNKS + 1,)),
        ],
        compiler_params=pltpu.CompilerParams(
            collective_id=0, has_side_effects=True, vmem_limit_bytes=63 * 1024 * 1024
        ),
    )(x_rows, g_rows, gate, up, down)


def per_device(tokens, ids, weights, out_grad, gate_weight, up_weight, down_weight):
    experts = lax.axis_size("expert")
    n_dp = lax.axis_size("dp")
    tok_rows, model = tokens.shape
    width = model // n_dp
    slots = min(tok_rows, 3 * tok_rows * ids.shape[1] // (2 * experts))
    gate, up, down = gate_weight[0], up_weight[0], down_weight[0]

    table = route_table(ids, weights, experts)
    whole, grad, tab = dispatch(tokens, out_grad, table)
    x_rows, g_rows = pick_rows(whole, slots, experts, n_dp, tok_rows, width)

    back, terms = exchange(x_rows, g_rows, gate, up, down, experts, n_dp)
    hid, gterm, uterm = terms[0], terms[1], terms[2]

    gate_grad = dot32(x_rows, gterm, ((0,), (0,))).astype(BF)[None]
    up_grad = dot32(x_rows, uterm, ((0,), (0,))).astype(BF)[None]
    down_grad = dot32(hid, g_rows, ((0,), (0,))).astype(BF)[None]

    mixed, tgrad, route = combine(back, ids, grad, tab, slots, experts, n_dp, tok_rows, width)
    return (mixed, tgrad, route, gate_grad, up_grad, down_grad)


def solution(mesh):
    rows = P(("dp", "expert"), None)
    weights = (P("expert", "dp", None), P("expert", "dp", None), P("expert", None, "dp"))
    return jax.shard_map(
        per_device,
        mesh=mesh,
        in_specs=(rows, rows, rows, rows) + weights,
        out_specs=(rows, rows, rows) + weights,
        check_vma=False,
    )
```

```python
import functools

import jax
import jax.numpy as jnp
from jax import lax
from jax.experimental import pallas as pl
from jax.experimental.pallas import tpu as pltpu
from jax.sharding import PartitionSpec as P

BF = jnp.bfloat16
F32 = jnp.float32
LANES = 128


def dot32(a, b, dims):
    return lax.dot_general(a, b, (dims, ((), ())), preferred_element_type=F32)


def route_table(ids, weights, experts):
    onehot = (ids[:, :, None] == jnp.arange(experts, dtype=jnp.int32)).astype(jnp.int32)
    chosen = jnp.sum(onehot, axis=1)
    place = jnp.cumsum(chosen, axis=0) * chosen
    dense = jnp.sum(onehot.astype(F32) * weights[:, :, None], axis=1)
    high = lax.reduce_precision(dense, 8, 7)
    middle = lax.reduce_precision(dense - high, 8, 7)
    low = dense - high - middle
    return jnp.concatenate([place.astype(F32), high, middle, low], axis=1).astype(BF)


def combine(back, ids, grad, tab, slots, experts, n_dp, tok_rows, width):
    tab = tab.astype(F32)
    toks = n_dp * tok_rows
    place = tab[:, :experts]
    weight = tab[:, experts : 2 * experts] + tab[:, 2 * experts : 3 * experts] + tab[:, 3 * experts : 4 * experts]
    row = jnp.arange(n_dp * slots, dtype=jnp.int32)
    tok = jnp.arange(toks, dtype=jnp.int32)
    same = (row[None, :] // slots) == (tok[:, None] // tok_rows)
    hit = same[:, None, :] & (place[:, :, None] == (row % slots + 1).astype(F32))
    flat = hit.reshape(toks, -1)
    scaled = jnp.where(hit, weight[:, :, None], 0.0).reshape(toks, -1)
    out_rows = back[:, :width]
    in_rows = back[:, width:]
    mixed = lax.dot_general(
        scaled, out_rows.astype(F32), (((1,), (0,)), ((), ())), precision=lax.Precision.HIGHEST
    )
    tgrad = dot32(flat.astype(BF), in_rows, ((1,), (0,)))
    dots = dot32(grad, out_rows, ((1,), (1,)))
    route = jnp.sum(jnp.where(hit, dots.reshape(hit.shape), 0.0), axis=2)
    both = jnp.concatenate([mixed, tgrad], axis=1).astype(BF).reshape(n_dp, tok_rows, 2 * width)
    both = lax.all_to_all(both, "dp", 0, 0, tiled=True)
    route = jnp.sum(lax.all_to_all(route.reshape(n_dp, tok_rows, experts), "dp", 0, 0, tiled=True), axis=0)
    both = both.transpose(1, 0, 2)
    mixed = both[:, :, :width].reshape(tok_rows, n_dp * width)
    tgrad = both[:, :, width:].reshape(tok_rows, n_dp * width)
    onehot = ids[:, :, None] == jnp.arange(experts, dtype=jnp.int32)
    route = jnp.sum(jnp.where(onehot, route[:, None, :], 0.0), axis=2)
    return mixed, tgrad, route


CHUNKS = 4
SIDE = 4
ORDER = (0, 1, 3, 2)
MESH = pl.DeviceIdType.MESH


def exchange_kernel(
    slots, tok_ref, grad_ref, tab_ref, gate_ref, up_ref, down_ref,
    back_ref, whole_ref, gate_out, up_out, down_out,
    blk, x_s, xt_s, g_s, hid_t, part, own, in_half, in_full, terms, rows_out, stage_a, stage_b,
    ring_send, ring_recv, ret_send, ret_recv, a2a_send, a2a_recv, ag_send, ag_recv,
    pair_send, pair_recv, local_sem, stage_sem,
):
    n_dp = lax.axis_size("dp")
    experts = lax.axis_size("expert")
    d = lax.axis_index("dp")
    e = lax.axis_index("expert")
    y = e // (2 * SIDE)
    z = (e // 2) % SIDE
    c = e % 2
    tok_rows = tok_ref.shape[0]
    toks = n_dp * tok_rows
    slots_dp = n_dp * slots
    group = experts // CHUNKS
    chunk = group * slots_dp
    half = chunk // 2
    quarter = own.shape[3]
    width = gate_ref.shape[0]
    to = ((d + n_dp - 1) % n_dp, (d + 1) % n_dp)

    barrier = pltpu.get_barrier_semaphore()
    for m in range(1, n_dp):
        pl.semaphore_signal(barrier, inc=1, device_id={"dp": (d + m) % n_dp}, device_id_type=MESH)

    def greet(step, carry):
        pl.semaphore_signal(
            barrier, inc=1, device_id={"expert": (e + step) % experts}, device_id_type=MESH
        )
        return carry

    lax.fori_loop(1, experts, greet, 0)
    pl.semaphore_wait(barrier, experts + n_dp - 2)

    sends = []

    def launch(item):
        item.start()
        sends.append(item)

    def spot(da, db, s):
        return db * group + s * SIDE + da

    def block(p, h=None):
        if h is None:
            return whole_ref.at[pl.ds(pl.multiple_of(p * toks, toks), toks), :]
        rows = toks // 2
        return whole_ref.at[pl.ds(pl.multiple_of(p * toks + h * rows, rows), rows), :]

    def to_slice(m, number):
        q = (d + m) % n_dp
        rows = pl.ds(pl.multiple_of((c * SIDE) * toks + d * tok_rows, tok_rows), tok_rows)
        cols = pl.ds(pl.multiple_of(q * width, LANES), width)
        source = (tok_ref.at[:, cols], grad_ref.at[:, cols], tab_ref)[number]
        target = whole_ref.at[rows, pl.ds(number * width, LANES if number == 2 else width)]
        if m == 0:
            return pltpu.make_async_copy(source, target, local_sem.at[number])
        return pltpu.make_async_remote_copy(
            src_ref=source, dst_ref=target, send_sem=a2a_send.at[m - 1, number],
            recv_sem=a2a_recv.at[m - 1, number], device_id={"dp": q}, device_id_type=MESH,
        )

    def from_slice(m, number):
        rows = pl.ds(pl.multiple_of((c * SIDE) * toks + ((d + n_dp - m) % n_dp) * tok_rows, tok_rows), tok_rows)
        ref = whole_ref.at[rows, pl.ds(number * width, LANES if number == 2 else width)]
        return pltpu.make_async_remote_copy(
            src_ref=ref, dst_ref=ref, send_sem=a2a_send.at[m - 1, number],
            recv_sem=a2a_recv.at[m - 1, number], device_id={"dp": (d + m) % n_dp}, device_id_type=MESH,
        )

    def ag_copy_to(axis, way, da, db, h):
        step = SIDE - 1 if way == 0 else 1
        seen = 1 if way == 0 else SIDE - 1
        da2 = (da + seen) % SIDE if axis == 0 else da
        db2 = (db + seen) % SIDE if axis == 1 else db
        along_y = 1 - c if axis == 0 else c
        y2 = (y + step * along_y) % SIDE
        z2 = (z + step * (1 - along_y)) % SIDE
        p2 = spot(da2, db2, c)
        return pltpu.make_async_remote_copy(
            src_ref=block(spot(da, db, c), h),
            dst_ref=block(p2, h),
            send_sem=ag_send.at[da * SIDE + db, axis * 2 + way, h],
            recv_sem=ag_recv.at[da2 * SIDE + db2, h],
            device_id={"expert": (y2 * SIDE + z2) * 2 + c},
            device_id_type=MESH,
        )

    def ag_wait(da, db, h):
        ref = block(spot(da, db, c), h)
        pltpu.make_async_remote_copy(
            src_ref=ref, dst_ref=ref, send_sem=ag_send.at[0, 0, 0], recv_sem=ag_recv.at[da * SIDE + db, h],
            device_id={"expert": (e + 1) % experts}, device_id_type=MESH,
        ).wait_recv()

    def pair_copy(da, db, s):
        ref = block(spot(da, db, s))
        return pltpu.make_async_remote_copy(
            src_ref=ref, dst_ref=ref, send_sem=pair_send.at[da * SIDE + db], recv_sem=pair_recv.at[da * SIDE + db],
            device_id={"expert": e + 1 - 2 * c}, device_id_type=MESH,
        )

    def spread(axis, da, db):
        for way, h in ((0, 0), (1, 1), (0, 1), (1, 0)):
            launch(ag_copy_to(axis, way, da, db, h))

    def slices():
        for m in range(n_dp):
            for number in range(3):
                to_slice(m, number).start()
        for number in range(3):
            to_slice(0, number).wait()
            for m in range(1, n_dp):
                from_slice(m, number).wait_recv()

    def first_phase():
        spread(0, 0, 0)
        launch(pair_copy(0, 0, c))
        ag_wait(1, 0, 0)
        launch(ag_copy_to(0, 0, 1, 0, 0))
        ag_wait(3, 0, 1)
        launch(ag_copy_to(0, 1, 3, 0, 1))
        spread(1, 0, 0)
        for da in (1, 3):
            ag_wait(da, 0, 1 if da == 1 else 0)
            launch(pair_copy(da, 0, c))
            spread(1, da, 0)
        ag_wait(2, 0, 0)
        ag_wait(2, 0, 1)
        launch(pair_copy(2, 0, c))
        spread(1, 2, 0)

    def second_phase(da):
        ag_wait(da, 1, 0)
        launch(ag_copy_to(1, 0, da, 1, 0))
        ag_wait(da, 3, 1)
        launch(ag_copy_to(1, 1, da, 3, 1))
        ag_wait(da, 1, 1)
        launch(pair_copy(da, 1, c))
        ag_wait(da, 3, 0)
        launch(pair_copy(da, 3, c))

    def third_phase(da):
        ag_wait(da, 2, 0)
        ag_wait(da, 2, 1)
        launch(pair_copy(da, 2, c))

    def take_chunk(k):
        db = ORDER[k]
        for da in range(SIDE):
            pair_copy(da, db, 1 - c).wait_recv()
        load = pltpu.make_async_copy(
            whole_ref.at[pl.ds(db * group * toks, group * toks), :], blk, local_sem.at[3]
        )
        load.start()
        load.wait()
        pair_rows = 2 * slots_dp
        pair_toks = 2 * toks

        def one(i, carry):
            span = pl.ds(pl.multiple_of(i * pair_toks, pair_toks), pair_toks)
            line = lax.broadcasted_iota(jnp.int32, (16, LANES), 0)
            lane = lax.broadcasted_iota(jnp.int32, (16, LANES), 1)
            want = jnp.where((lane == line * experts + e) & (line < 4), 1.0, 0.0).astype(BF)
            found = dot32(want, blk[span, 2 * width :], ((1,), (1,)))
            place = found[0:1, :]
            scale = found[1:2, :] + found[2:3, :] + found[3:4, :]
            token = lax.broadcasted_iota(jnp.int32, (1, pair_toks), 1)
            base = (lax.shift_right_logical(token, tok_rows.bit_length() - 1) * slots).astype(F32)
            goal = jnp.where(place > 0.0, base + place - 1.0, -1.0)
            row = lax.broadcasted_iota(jnp.int32, (pair_rows, pair_toks), 0).astype(F32)
            hit = row == goal
            picked = jnp.dot(
                jnp.where(hit, 1.0, 0.0).astype(BF), blk[span, : 2 * width], preferred_element_type=F32
            )
            scales = jnp.sum(jnp.where(hit, scale, 0.0), axis=1, keepdims=True)
            x_s[pl.ds(pl.multiple_of(i * pair_rows, pair_rows), pair_rows), :] = picked[:, :width].astype(BF)
            g_s[pl.ds(pl.multiple_of(k * chunk + i * pair_rows, pair_rows), pair_rows), :] = (
                picked[:, width:] * scales
            ).astype(BF)
            return carry

        lax.fori_loop(0, group // 2, one, 0)

    def rows_of(k, part_half=None):
        if part_half is None:
            return pl.ds(k * chunk, chunk)
        return pl.ds(k * chunk + part_half * half, half)

    def cols_of(q):
        return pl.ds(pl.multiple_of(q * quarter, quarter), quarter)

    def copy(k, way, number, source, target):
        return pltpu.make_async_remote_copy(
            src_ref=source,
            dst_ref=target,
            send_sem=ring_send.at[k, way, number],
            recv_sem=ring_recv.at[k, way, number],
            device_id={"dp": to[way]},
            device_id_type=MESH,
        )

    def toward(k, way):
        return part.at[k, 2 if way == 0 else 0]

    def halves(ref, h):
        return ref.at[:, pl.ds(h * half, half), :]

    def rs_copy(k, way, number):
        if number == 0:
            return copy(k, way, 0, halves(part.at[k, 1], way), in_half.at[k, way])
        h = way if number == 2 else 1 - way
        return copy(k, way, number, halves(toward(k, way), h), halves(in_full.at[k, way], h))

    def ag_copy(k, way, number):
        if number == 5:
            q = (d + 1) % n_dp if way == 0 else (d + n_dp - 1) % n_dp
            h = way
        else:
            q = d
            h = way if number == 3 else 1 - way
        ref = terms.at[:, rows_of(k, h), cols_of(q)]
        return copy(k, way, number, ref, ref)

    def ag_arrival(k, way, number):
        src = (d + 1) % n_dp if way == 0 else (d + n_dp - 1) % n_dp
        q = (d + 2) % n_dp if number == 5 else src
        h = way if number in (3, 5) else 1 - way
        ref = terms.at[:, rows_of(k, h), cols_of(q)]
        return copy(k, way, number, ref, ref)

    def partial(k, q, i):
        if i == 0:
            return jnp.dot(x_s[...], gate_ref[:, cols_of(q)], preferred_element_type=F32)
        if i == 1:
            return jnp.dot(x_s[...], up_ref[:, cols_of(q)], preferred_element_type=F32)
        return dot32(g_s[rows_of(k), :], down_ref[cols_of(q), :], ((1,), (1,)))

    def stage0(k):
        def one(step, carry):
            m = (step + 1) % (n_dp - 1)
            q = (d + m + 1) % n_dp
            for i in range(3):
                part[k, m, i] = partial(k, q, i).astype(BF)
            return carry

        lax.fori_loop(0, n_dp - 1, one, 0)
        for way in range(2):
            rs_copy(k, way, 0).start()
        for way in range(2):
            rs_copy(k, way, 1).start()
        for i in range(3):
            own[k, i] = partial(k, d, i)
        xt_s[:, rows_of(k)] = x_s[...].T

    def stage1(k):
        for way in range(2):
            rs_copy(k, way, 0).wait_recv()
            m = 2 if way == 0 else 0
            for i in range(3):
                span = pl.ds(way * half, half)
                total = part[k, m, i, span, :].astype(F32) + in_half[k, way, i].astype(F32)
                part[k, m, i, span, :] = total.astype(BF)
            rs_copy(k, way, 2).start()

    def stage2(k):
        for number in (1, 2):
            for way in range(2):
                rs_copy(k, way, number).wait_recv()

        def total(i, span):
            return own[k, i, span, :] + in_full[k, 0, i, span, :].astype(F32) + in_full[k, 1, i, span, :].astype(F32)

        step_rows = half // 2

        def act(step, carry):
            span = pl.ds(pl.multiple_of(step * step_rows, step_rows), step_rows)
            gate = total(0, span)
            up = total(1, span)
            hgrad = total(2, span)
            sig = jax.nn.sigmoid(gate)
            val = gate * sig
            slope = sig * (1.0 + gate * (1.0 - sig))
            target = pl.ds(pl.multiple_of(k * chunk + step * step_rows, step_rows), step_rows)
            terms[0, target, cols_of(d)] = (val * up).astype(BF)
            terms[1, target, cols_of(d)] = (hgrad * up * slope).astype(BF)
            terms[2, target, cols_of(d)] = (hgrad * val).astype(BF)
            return carry

        lax.fori_loop(0, chunk // step_rows, act, 0)
        for number in (3, 4):
            for way in range(2):
                ag_copy(k, way, number).start()

    def stage3(k):
        for way in range(2):
            ag_arrival(k, way, 3).wait_recv()
            ag_copy(k, way, 5).start()

    def home(p):
        return pl.ds(pl.multiple_of(p * slots_dp, slots_dp), slots_dp)

    def back_copy(k, i):
        db = ORDER[k]
        s = i // SIDE
        da = i % SIDE
        y2 = (y + da * (1 - s) + db * s) % SIDE
        z2 = (z + db * (1 - s) + da * s) % SIDE
        j = (y2 * SIDE + z2) * 2 + s
        return pltpu.make_async_remote_copy(
            src_ref=rows_out.at[home(k * group + i), :],
            dst_ref=back_ref.at[home(e), :],
            send_sem=ret_send.at[k * group + i],
            recv_sem=ret_recv.at[e],
            device_id={"expert": j},
            device_id_type=MESH,
        )

    def self_copy():
        return pltpu.make_async_copy(
            rows_out.at[home(c * SIDE), :], back_ref.at[home(e), :], local_sem.at[4]
        )

    def each_back(k, act):
        def one(step, carry):
            act(back_copy(k, (c * SIDE + step) % group))
            return carry

        lax.fori_loop(1 if k == 0 else 0, group, one, 0)

    def stage4(k):
        for way in range(2):
            ag_arrival(k, way, 4).wait_recv()
        for way in range(2):
            ag_arrival(k, way, 5).wait_recv()

        def one(h, carry):
            span = pl.ds(pl.multiple_of(k * chunk + h * half, half), half)
            rows_out[span, :width] = jnp.dot(
                terms[0, span, :], down_ref[...], preferred_element_type=F32
            ).astype(BF)
            rows_out[span, width:] = (
                dot32(terms[1, span, :], gate_ref[...], ((1,), (1,)))
                + dot32(terms[2, span, :], up_ref[...], ((1,), (1,)))
            ).astype(BF)
            return carry

        lax.fori_loop(0, 2, one, 0)
        if k == 0:
            self_copy().start()
        each_back(k, lambda item: item.start())
        hid_t[:, rows_of(k)] = terms[0, rows_of(k), :].T

    def weight_grads():
        span = stage_a.shape[2]
        tall = stage_b.shape[1]

        def out_copy(kind, i, slot):
            if kind == 2:
                target = down_out.at[pl.ds(pl.multiple_of(i * tall, tall), tall), :]
                return pltpu.make_async_copy(stage_b.at[slot], target, stage_sem.at[kind, slot])
            target = (gate_out, up_out)[kind].at[:, pl.ds(pl.multiple_of(i * span, span), span)]
            return pltpu.make_async_copy(stage_a.at[slot], target, stage_sem.at[kind, slot])

        for kind in range(3):
            count = gate_ref.shape[1] // (tall if kind == 2 else span)

            def one(i, carry, kind=kind):
                slot = i % 2

                @pl.when(i >= 2)
                def _():
                    out_copy(kind, i - 2, slot).wait()

                if kind == 2:
                    left = hid_t[pl.ds(pl.multiple_of(i * tall, tall), tall), :]
                    stage_b[slot] = jnp.dot(left, g_s[...], preferred_element_type=F32).astype(BF)
                else:
                    right = terms[1 + kind, :, pl.ds(pl.multiple_of(i * span, span), span)]
                    stage_a[slot] = jnp.dot(xt_s[...], right, preferred_element_type=F32).astype(BF)
                out_copy(kind, i, slot).start()
                return carry

            lax.fori_loop(0, count, one, 0)
            out_copy(kind, count - 2, count % 2).wait()
            out_copy(kind, count - 1, (count - 1) % 2).wait()

    slices()
    first_phase()
    for t in range(CHUNKS + 4):
        if 0 <= t - 1 < CHUNKS:
            stage1(t - 1)
        if t == 1:
            second_phase(3)
            second_phase(2)
        if 0 <= t - 2 < CHUNKS:
            stage2(t - 2)
        if 0 <= t - 3 < CHUNKS:
            stage3(t - 3)
        if t == 2:
            for da in (0, 1, 3, 2):
                third_phase(da)
        if t < CHUNKS:
            take_chunk(t)
            stage0(t)
        if t == 0:
            second_phase(0)
            second_phase(1)
        if 0 <= t - 4 < CHUNKS:
            stage4(t - 4)
    weight_grads()

    for m in range(1, n_dp):
        for number in range(3):
            to_slice(m, number).wait_send()
    for item in sends:
        item.wait_send()
    for k in range(CHUNKS):
        for way in range(2):
            for number in range(3):
                rs_copy(k, way, number).wait_send()
                ag_copy(k, way, number + 3).wait_send()
        each_back(k, lambda item: item.wait_send())
    self_copy().wait()

    def arrived(step, carry):
        s = (e + step) % experts
        ref = back_ref.at[home(s), :]
        pltpu.make_async_remote_copy(
            src_ref=ref, dst_ref=ref, send_sem=ret_send.at[s], recv_sem=ret_recv.at[s],
            device_id={"expert": s}, device_id_type=MESH,
        ).wait_recv()
        return carry

    lax.fori_loop(1, experts, arrived, 0)


def exchange(tokens, out_grad, table, gate, up, down, slots, experts, n_dp):
    width, hidden = gate.shape
    toks = n_dp * tokens.shape[0]
    rows = experts * n_dp * slots
    quarter = hidden // n_dp
    chunk = rows // CHUNKS
    group = experts // CHUNKS
    dma = pltpu.SemaphoreType.DMA
    anywhere = pl.BlockSpec(memory_space=pl.ANY)
    return pl.pallas_call(
        functools.partial(exchange_kernel, slots),
        out_shape=(
            jax.ShapeDtypeStruct((rows, 2 * width), BF),
            jax.ShapeDtypeStruct((experts * toks, 2 * width + LANES), BF),
            jax.ShapeDtypeStruct((width, hidden), BF),
            jax.ShapeDtypeStruct((width, hidden), BF),
            jax.ShapeDtypeStruct((hidden, width), BF),
        ),
        in_specs=[pl.BlockSpec(memory_space=pltpu.VMEM)] * 6,
        out_specs=(anywhere,) * 5,
        scratch_shapes=[
            pltpu.VMEM((group * toks, 2 * width + LANES), BF),
            pltpu.VMEM((chunk, width), BF),
            pltpu.VMEM((width, rows), BF),
            pltpu.VMEM((rows, width), BF),
            pltpu.VMEM((hidden, rows), BF),
            pltpu.VMEM((CHUNKS, n_dp - 1, 3, chunk, quarter), BF),
            pltpu.VMEM((CHUNKS, 3, chunk, quarter), F32),
            pltpu.VMEM((CHUNKS, 2, 3, chunk // 2, quarter), BF),
            pltpu.VMEM((CHUNKS, 2, 3, chunk, quarter), BF),
            pltpu.VMEM((3, rows, hidden), BF),
            pltpu.VMEM((rows, 2 * width), BF),
            pltpu.VMEM((2, width, quarter), BF),
            pltpu.VMEM((2, quarter, width), BF),
            dma((CHUNKS, 2, 6)),
            dma((CHUNKS, 2, 6)),
            dma((experts,)),
            dma((experts,)),
            dma((n_dp - 1, 3)),
            dma((n_dp - 1, 3)),
            dma((SIDE * SIDE, 4, 2)),
            dma((SIDE * SIDE, 2)),
            dma((SIDE * SIDE,)),
            dma((SIDE * SIDE,)),
            dma((5,)),
            dma((3, 2)),
        ],
        compiler_params=pltpu.CompilerParams(
            collective_id=0, has_side_effects=True, vmem_limit_bytes=63 * 1024 * 1024
        ),
    )(tokens, out_grad, table, gate, up, down)


def per_device(tokens, ids, weights, out_grad, gate_weight, up_weight, down_weight):
    experts = lax.axis_size("expert")
    n_dp = lax.axis_size("dp")
    tok_rows, model = tokens.shape
    width = model // n_dp
    slots = min(tok_rows, 3 * tok_rows * ids.shape[1] // (2 * experts))
    gate, up, down = gate_weight[0], up_weight[0], down_weight[0]

    table = route_table(ids, weights, experts)
    back, whole, gate_grad, up_grad, down_grad = exchange(
        tokens, out_grad, table, gate, up, down, slots, experts, n_dp
    )
    mine = (lax.axis_index("expert") % 2) * SIDE * n_dp * tok_rows
    block = lax.dynamic_slice_in_dim(whole, mine, n_dp * tok_rows, 0)
    grad, tab = block[:, width : 2 * width], block[:, 2 * width :]
    mixed, tgrad, route = combine(back, ids, grad, tab, slots, experts, n_dp, tok_rows, width)
    return (mixed, tgrad, route, gate_grad[None], up_grad[None], down_grad[None])


def solution(mesh):
    rows = P(("dp", "expert"), None)
    weights = (P("expert", "dp", None), P("expert", "dp", None), P("expert", None, "dp"))
    return jax.shard_map(
        per_device,
        mesh=mesh,
        in_specs=(rows, rows, rows, rows) + weights,
        out_specs=(rows, rows, rows) + weights,
        check_vma=False,
    )
```

```python
import jax
import jax.numpy as jnp
from jax import lax
from jax.experimental import pallas as pl
from jax.experimental.pallas import tpu as pltpu
from jax.sharding import PartitionSpec as P

BF = jnp.bfloat16
F32 = jnp.float32
LANES = 128
SIDE = 4
GROUP = 8
CHUNKS = ((0, 4), (8, 8), (24, 8), (16, 8), (4, 4))
MESH = pl.DeviceIdType.MESH


def dot32(a, b, dims, precision=None):
    return lax.dot_general(a, b, (dims, ((), ())), precision=precision, preferred_element_type=F32)


def moe_kernel(
    tok_ref, grad_ref, ids_ref, wts_ref, gate_ref, up_ref, down_ref,
    mixed_out, tgrad_out, route_out, gate_out, up_out, down_out, back_ref, whole_ref,
    tab_s, mine, blk, x_s, xt_s, g_s, hid_t, part, own, in_half, in_full, terms, rows_out, stage_a, stage_b,
    bk, mixed_acc, tgrad_acc, route_acc, final_v, route_in,
    ring_send, ring_recv, ret_send, ret_recv, a2a_send, a2a_recv, ag_send, ag_recv,
    pair_send, pair_recv, local_sem, stage_sem, fin_send, fin_recv,
):
    n_dp = lax.axis_size("dp")
    experts = lax.axis_size("expert")
    d = lax.axis_index("dp")
    e = lax.axis_index("expert")
    y = e // (2 * SIDE)
    z = (e // 2) % SIDE
    c = e % 2
    tok_rows, top = ids_ref.shape
    toks = n_dp * tok_rows
    tok_bits = tok_rows.bit_length() - 1
    slots_dp = rows_out.shape[0] // experts
    slots = slots_dp // n_dp
    quarter = own.shape[2]
    width = gate_ref.shape[0]
    to = ((d + n_dp - 1) % n_dp, (d + 1) % n_dp)

    barrier = pltpu.get_barrier_semaphore()
    for m in range(1, n_dp):
        pl.semaphore_signal(barrier, inc=1, device_id={"dp": (d + m) % n_dp}, device_id_type=MESH)

    def greet(step, carry):
        pl.semaphore_signal(
            barrier, inc=1, device_id={"expert": (e + step) % experts}, device_id_type=MESH
        )
        return carry

    lax.fori_loop(1, experts, greet, 0)

    def make_table():
        lane = lax.broadcasted_iota(jnp.int32, (tok_rows, LANES), 1)
        name = lane & (experts - 1)
        kind = lax.shift_right_logical(lane, experts.bit_length() - 1)
        chosen = jnp.zeros((tok_rows, LANES), F32)
        weight = jnp.zeros((tok_rows, LANES), F32)
        for k in range(top):
            same = ids_ref[:, k : k + 1] == name
            chosen += jnp.where(same, 1.0, 0.0)
            weight += jnp.where(same, wts_ref[:, k : k + 1], 0.0)
        row = lax.broadcasted_iota(jnp.int32, (tok_rows, tok_rows), 0)
        col = lax.broadcasted_iota(jnp.int32, (tok_rows, tok_rows), 1)
        below = jnp.where(row >= col, 1.0, 0.0).astype(BF)
        place = jnp.dot(below, chosen.astype(BF), preferred_element_type=F32) * chosen
        high = weight.astype(BF).astype(F32)
        middle = (weight - high).astype(BF).astype(F32)
        low = weight - high - middle
        value = jnp.where(kind == 0, place, jnp.where(kind == 1, high, jnp.where(kind == 2, middle, low)))
        tab_s[...] = value.astype(BF)

    make_table()
    pl.semaphore_wait(barrier, experts + n_dp - 2)

    sends = []

    def launch(item):
        item.start()
        sends.append(item)

    def block(p, h=None):
        if h is None:
            return whole_ref.at[pl.ds(p * toks, toks), :]
        rows = toks // 2
        return whole_ref.at[pl.ds(p * toks + h * rows, rows), :]

    def own_slice(src, number):
        rows = pl.ds(pl.multiple_of(src * tok_rows, tok_rows), tok_rows)
        return whole_ref.at[rows, pl.ds(number * width, LANES if number == 2 else width)]

    def to_slice(m, number):
        q = (d + m) % n_dp
        cols = pl.ds(pl.multiple_of(q * width, LANES), width)
        source = tab_s if number == 2 else (tok_ref, grad_ref)[number].at[:, cols]
        target = own_slice(d, number)
        if m == 0:
            return pltpu.make_async_copy(source, target, local_sem.at[number])
        return pltpu.make_async_remote_copy(
            src_ref=source, dst_ref=target, send_sem=a2a_send.at[m - 1, number],
            recv_sem=a2a_recv.at[m - 1, number], device_id={"dp": q}, device_id_type=MESH,
        )

    def from_slice(m, number):
        ref = own_slice((d + n_dp - m) % n_dp, number)
        return pltpu.make_async_remote_copy(
            src_ref=ref, dst_ref=ref, send_sem=a2a_send.at[m - 1, number],
            recv_sem=a2a_recv.at[m - 1, number], device_id={"dp": (d + m) % n_dp}, device_id_type=MESH,
        )

    def spot(da, db, rel):
        return db * GROUP + rel * SIDE + da

    def ag_copy_to(axis, way, da, db, h):
        step = SIDE - 1 if way == 0 else 1
        seen = 1 if way == 0 else SIDE - 1
        da2 = (da + seen) % SIDE if axis == 0 else da
        db2 = (db + seen) % SIDE if axis == 1 else db
        along_y = 1 - c if axis == 0 else c
        y2 = (y + step * along_y) % SIDE
        z2 = (z + step * (1 - along_y)) % SIDE
        return pltpu.make_async_remote_copy(
            src_ref=block(spot(da, db, 0), h),
            dst_ref=block(spot(da2, db2, 0), h),
            send_sem=ag_send.at[da * SIDE + db, axis * 2 + way, h],
            recv_sem=ag_recv.at[da2 * SIDE + db2, h],
            device_id={"expert": (y2 * SIDE + z2) * 2 + c},
            device_id_type=MESH,
        )

    def ag_wait(da, db, h):
        ref = block(spot(da, db, 0), h)
        pltpu.make_async_remote_copy(
            src_ref=ref, dst_ref=ref, send_sem=ag_send.at[0, 0, 0], recv_sem=ag_recv.at[da * SIDE + db, h],
            device_id={"expert": (e + 1) % experts}, device_id_type=MESH,
        ).wait_recv()

    def pair_copy(da, db):
        return pltpu.make_async_remote_copy(
            src_ref=block(spot(da, db, 0)), dst_ref=block(spot(da, db, 1)),
            send_sem=pair_send.at[da * SIDE + db], recv_sem=pair_recv.at[da * SIDE + db],
            device_id={"expert": e + 1 - 2 * c}, device_id_type=MESH,
        )

    def spread(axis, da, db):
        for way, h in ((0, 0), (1, 1), (0, 1), (1, 0)):
            launch(ag_copy_to(axis, way, da, db, h))

    def slices():
        for m in (1, 3, 2, 0):
            for number in range(3):
                to_slice(m, number).start()
        for number in range(3):
            to_slice(0, number).wait()
            for m in range(1, n_dp):
                from_slice(m, number).wait_recv()

    def mine_copy():
        return pltpu.make_async_copy(block(0), mine, local_sem.at[5])

    def first_phase():
        spread(0, 0, 0)
        launch(pair_copy(0, 0))
        mine_copy().start()
        ag_wait(1, 0, 0)
        launch(ag_copy_to(0, 0, 1, 0, 0))
        ag_wait(3, 0, 1)
        launch(ag_copy_to(0, 1, 3, 0, 1))
        spread(1, 0, 0)
        for da in (1, 3):
            ag_wait(da, 0, 1 if da == 1 else 0)
            launch(pair_copy(da, 0))
            spread(1, da, 0)
        ag_wait(2, 0, 0)
        ag_wait(2, 0, 1)
        launch(pair_copy(2, 0))
        spread(1, 2, 0)
        mine_copy().wait()

    def second_phase(da):
        ag_wait(da, 1, 0)
        launch(ag_copy_to(1, 0, da, 1, 0))
        ag_wait(da, 3, 1)
        launch(ag_copy_to(1, 1, da, 3, 1))
        ag_wait(da, 1, 1)
        launch(pair_copy(da, 1))
        ag_wait(da, 3, 0)
        launch(pair_copy(da, 3))

    def third_phase(da):
        ag_wait(da, 2, 0)
        ag_wait(da, 2, 1)
        launch(pair_copy(da, 2))

    def size_of(k):
        return CHUNKS[k][1] * slots_dp

    def rows_of(k, part_half=None):
        start = CHUNKS[k][0] * slots_dp
        if part_half is None:
            return pl.ds(start, size_of(k))
        return pl.ds(start + part_half * (size_of(k) // 2), size_of(k) // 2)

    def half_rows(k):
        return pl.ds(CHUNKS[k][0] * slots_dp // 2, size_of(k) // 2)

    def cols_of(q):
        return pl.ds(pl.multiple_of(q * quarter, quarter), quarter)

    def take_chunk(k):
        first, count = CHUNKS[k]
        for p in range(first, first + count):
            if (p // SIDE) % 2 == 1:
                pair_copy(p % SIDE, p // GROUP).wait_recv()
        load = pltpu.make_async_copy(
            whole_ref.at[pl.ds(first * toks, count * toks), :], blk.at[pl.ds(0, count * toks), :], local_sem.at[3]
        )
        load.start()
        load.wait()
        pair_rows = 2 * slots_dp
        pair_toks = 2 * toks

        def one(i, carry):
            span = pl.ds(pl.multiple_of(i * pair_toks, pair_toks), pair_toks)
            line = lax.broadcasted_iota(jnp.int32, (16, LANES), 0)
            lane = lax.broadcasted_iota(jnp.int32, (16, LANES), 1)
            want = jnp.where((lane == line * experts + e) & (line < 4), 1.0, 0.0).astype(BF)
            found = dot32(want, blk[span, 2 * width :], ((1,), (1,)))
            place = found[0:1, :]
            scale = found[1:2, :] + found[2:3, :] + found[3:4, :]
            token = lax.broadcasted_iota(jnp.int32, (1, pair_toks), 1)
            base = (lax.shift_right_logical(token, tok_bits) * slots).astype(F32)
            goal = jnp.where(place > 0.0, base + place - 1.0, -1.0)
            row = lax.broadcasted_iota(jnp.int32, (pair_rows, pair_toks), 0).astype(F32)
            hit = row == goal
            picked = jnp.dot(
                jnp.where(hit, 1.0, 0.0).astype(BF), blk[span, : 2 * width], preferred_element_type=F32
            )
            scales = jnp.sum(jnp.where(hit, scale, 0.0), axis=1, keepdims=True)
            x_s[pl.ds(pl.multiple_of(i * pair_rows, pair_rows), pair_rows), :] = picked[:, :width].astype(BF)
            g_s[pl.ds(pl.multiple_of(first * slots_dp + i * pair_rows, pair_rows), pair_rows), :] = (
                picked[:, width:] * scales
            ).astype(BF)
            return carry

        lax.fori_loop(0, count // 2, one, 0)

    def copy(k, way, number, source, target):
        return pltpu.make_async_remote_copy(
            src_ref=source, dst_ref=target, send_sem=ring_send.at[k, way, number],
            recv_sem=ring_recv.at[k, way, number], device_id={"dp": to[way]}, device_id_type=MESH,
        )

    def toward(way):
        return part.at[2 if way == 0 else 0]

    def rs_copy(k, way, number):
        if number == 0:
            return copy(k, way, 0, part.at[1, :, rows_of(k, way), :], in_half.at[way, :, half_rows(k), :])
        h = way if number == 2 else 1 - way
        return copy(
            k, way, number, toward(way).at[:, rows_of(k, h), :], in_full.at[way, :, rows_of(k, h), :]
        )

    def ag_terms(k, way, number, q):
        h = way if number in (3, 5) else 1 - way
        ref = terms.at[:, rows_of(k, h), cols_of(q)]
        return copy(k, way, number, ref, ref)

    def ring_copy(k, way, number):
        return ag_terms(k, way, number, to[1 - way] if number == 5 else d)

    def ring_arrival(k, way, number):
        return ag_terms(k, way, number, (d + 2) % n_dp if number == 5 else to[1 - way])

    def partial(k, q, i):
        if i == 2:
            return dot32(g_s[rows_of(k), :], down_ref[cols_of(q), :], ((1,), (1,)))
        right = (gate_ref, up_ref)[i]
        return jnp.dot(x_s[pl.ds(0, size_of(k)), :], right[:, cols_of(q)], preferred_element_type=F32)

    def stage0(k):
        def one(step, carry):
            m = (step + 1) % (n_dp - 1)
            q = (d + m + 1) % n_dp
            for i in range(3):
                part[m, i, rows_of(k), :] = partial(k, q, i).astype(BF)
            return carry

        lax.fori_loop(0, n_dp - 1, one, 0)
        for number in range(2):
            for way in range(2):
                rs_copy(k, way, number).start()
        for i in range(3):
            own[i, rows_of(k), :] = partial(k, d, i)
        xt_s[:, rows_of(k)] = x_s[pl.ds(0, size_of(k)), :].T

    def stage1(k):
        for way in range(2):
            rs_copy(k, way, 0).wait_recv()
            m = 2 if way == 0 else 0
            for i in range(3):
                span = rows_of(k, way)
                total = part[m, i, span, :].astype(F32) + in_half[way, i, half_rows(k), :].astype(F32)
                part[m, i, span, :] = total.astype(BF)
            rs_copy(k, way, 2).start()

    def stage2(k):
        for number in (1, 2):
            for way in range(2):
                rs_copy(k, way, number).wait_recv()

        def total(i, span):
            return own[i, span, :] + in_full[0, i, span, :].astype(F32) + in_full[1, i, span, :].astype(F32)

        step_rows = 2 * slots_dp

        def act(step, carry):
            start = CHUNKS[k][0] * slots_dp + step * step_rows
            span = pl.ds(pl.multiple_of(start, step_rows), step_rows)
            gate = total(0, span)
            up = total(1, span)
            hgrad = total(2, span)
            sig = jax.nn.sigmoid(gate)
            val = gate * sig
            slope = sig * (1.0 + gate * (1.0 - sig))
            terms[0, span, cols_of(d)] = (val * up).astype(BF)
            terms[1, span, cols_of(d)] = (hgrad * up * slope).astype(BF)
            terms[2, span, cols_of(d)] = (hgrad * val).astype(BF)
            return carry

        lax.fori_loop(0, size_of(k) // step_rows, act, 0)
        for number in (3, 4):
            for way in range(2):
                ring_copy(k, way, number).start()

    def stage3(k):
        for way in range(2):
            ring_arrival(k, way, 3).wait_recv()
            ring_copy(k, way, 5).start()

    def home(p):
        return pl.ds(pl.multiple_of(p * slots_dp, slots_dp), slots_dp)

    def back_copy(k, i):
        db = CHUNKS[k][0] // GROUP
        p = CHUNKS[k][0] + i
        s = (c + p // SIDE) % 2
        da = p % SIDE
        y2 = (y + da * (1 - s) + db * s) % SIDE
        z2 = (z + db * (1 - s) + da * s) % SIDE
        return pltpu.make_async_remote_copy(
            src_ref=rows_out.at[home(p), :],
            dst_ref=back_ref.at[home(p), :],
            send_sem=ret_send.at[p],
            recv_sem=ret_recv.at[p],
            device_id={"expert": (y2 * SIDE + z2) * 2 + s},
            device_id_type=MESH,
        )

    def self_copy():
        return pltpu.make_async_copy(rows_out.at[home(0), :], back_ref.at[home(0), :], local_sem.at[4])

    def each_back(k, act):
        def one(i, carry):
            act(back_copy(k, i))
            return carry

        lax.fori_loop(1 if k == 0 else 0, CHUNKS[k][1], one, 0)

    def stage4(k):
        for number in (4, 5):
            for way in range(2):
                ring_arrival(k, way, number).wait_recv()
        half = size_of(k) // 2

        def one(h, carry):
            span = pl.ds(pl.multiple_of(CHUNKS[k][0] * slots_dp + h * half, half), half)
            rows_out[span, :width] = jnp.dot(
                terms[0, span, :], down_ref[...], preferred_element_type=F32
            ).astype(BF)
            rows_out[span, width:] = (
                dot32(terms[1, span, :], gate_ref[...], ((1,), (1,)))
                + dot32(terms[2, span, :], up_ref[...], ((1,), (1,)))
            ).astype(BF)
            return carry

        lax.fori_loop(0, 2, one, 0)
        if k == 0:
            self_copy().start()
        each_back(k, lambda item: item.start())
        hid_t[:, rows_of(k)] = terms[0, rows_of(k), :].T

    def fold(k):
        first, count = CHUNKS[k]
        rows = size_of(k)
        each_back(k, lambda item: item.wait_recv())
        if k == 0:
            self_copy().wait()
        load = pltpu.make_async_copy(back_ref.at[rows_of(k), :], bk.at[pl.ds(0, rows), :], local_sem.at[6])
        load.start()
        row = lax.broadcasted_iota(jnp.int32, (1, rows), 1)
        index = lax.shift_right_logical(row * (65536 // slots_dp + 1), 16)
        local = (row - index * slots_dp).astype(F32)
        p = first + index
        db = first // GROUP
        da = p & (SIDE - 1)
        core = (c + lax.shift_right_logical(p, 2)) & 1
        y2 = (y + 2 * SIDE - (da * (1 - c) + db * c)) & (SIDE - 1)
        z2 = (z + 2 * SIDE - (db * (1 - c) + da * c)) & (SIDE - 1)
        sender = (y2 * SIDE + z2) * 2 + core
        lane = lax.broadcasted_iota(jnp.int32, (LANES, rows), 0)
        names = [jnp.where(lane == kind * experts + sender, 1.0, 0.0) for kind in range(4)]
        table = mine[:, 2 * width :]
        found = [jnp.dot(table, name.astype(BF), preferred_element_type=F32) for name in names]
        token = lax.broadcasted_iota(jnp.int32, (toks, rows), 0)
        base = (lax.shift_right_logical(token, tok_bits) * slots).astype(F32)
        hit = (found[0] > 0.0) & (local == base + found[0] - 1.0)
        scaled = jnp.concatenate([jnp.where(hit, found[i], 0.0).astype(BF) for i in (1, 2, 3)], axis=0)
        once = jnp.where(hit, 1.0, 0.0).astype(BF)
        load.wait()
        outs = bk[pl.ds(0, rows), :width]
        three = jnp.dot(scaled, outs, preferred_element_type=F32)
        mixed = three[:toks] + three[toks : 2 * toks] + three[2 * toks :]
        tgrad = jnp.dot(once, bk[pl.ds(0, rows), width:], preferred_element_type=F32)
        dots = dot32(mine[:, width : 2 * width], outs, ((1,), (1,)))
        route = dot32(jnp.where(hit, dots, 0.0), names[0], ((1,), (1,)), lax.Precision.HIGHEST)
        if k == 0:
            mixed_acc[...] = mixed
            tgrad_acc[...] = tgrad
            route_acc[...] = route
        else:
            mixed_acc[...] += mixed
            tgrad_acc[...] += tgrad
            route_acc[...] += route

    def weight_grads():
        span = stage_a.shape[2]
        tall = stage_b.shape[1]

        def out_copy(kind, i, slot):
            if kind == 2:
                target = down_out.at[pl.ds(pl.multiple_of(i * tall, tall), tall), :]
                return pltpu.make_async_copy(stage_b.at[slot], target, stage_sem.at[kind, slot])
            target = (gate_out, up_out)[kind].at[:, pl.ds(pl.multiple_of(i * span, span), span)]
            return pltpu.make_async_copy(stage_a.at[slot], target, stage_sem.at[kind, slot])

        for kind in range(3):
            count = gate_ref.shape[1] // (tall if kind == 2 else span)

            def one(i, carry, kind=kind):
                slot = i % 2

                @pl.when(i >= 2)
                def _():
                    out_copy(kind, i - 2, slot).wait()

                if kind == 2:
                    left = hid_t[pl.ds(pl.multiple_of(i * tall, tall), tall), :]
                    stage_b[slot] = jnp.dot(left, g_s[...], preferred_element_type=F32).astype(BF)
                else:
                    right = terms[1 + kind, :, pl.ds(pl.multiple_of(i * span, span), span)]
                    stage_a[slot] = jnp.dot(xt_s[...], right, preferred_element_type=F32).astype(BF)
                out_copy(kind, i, slot).start()
                return carry

            lax.fori_loop(0, count, one, 0)
            out_copy(kind, count - 2, count % 2).wait()
            out_copy(kind, count - 1, (count - 1) % 2).wait()

    def final_copy(m, number):
        q = (d + m) % n_dp
        rows = pl.ds(pl.multiple_of(q * tok_rows, tok_rows), tok_rows)
        if number == 2:
            source, target = route_acc.at[rows, :], route_in.at[d]
        else:
            source = final_v.at[rows, pl.ds(number * width, width)]
            target = (mixed_out, tgrad_out)[number].at[:, pl.ds(pl.multiple_of(d * width, LANES), width)]
        if m == 0:
            return pltpu.make_async_copy(source, target, fin_send.at[m, number])
        return pltpu.make_async_remote_copy(
            src_ref=source, dst_ref=target, send_sem=fin_send.at[m, number],
            recv_sem=fin_recv.at[m - 1, number], device_id={"dp": q}, device_id_type=MESH,
        )

    def final_arrival(m, number):
        src = (d + n_dp - m) % n_dp
        if number == 2:
            ref = route_in.at[src]
        else:
            ref = (mixed_out, tgrad_out)[number].at[:, pl.ds(pl.multiple_of(src * width, LANES), width)]
        return pltpu.make_async_remote_copy(
            src_ref=ref, dst_ref=ref, send_sem=fin_send.at[m, number],
            recv_sem=fin_recv.at[m - 1, number], device_id={"dp": (d + m) % n_dp}, device_id_type=MESH,
        )

    def finish():
        final_v[:, :width] = mixed_acc[...].astype(BF)
        final_v[:, width:] = tgrad_acc[...].astype(BF)
        for m in (2, 1, 3, 0):
            for number in range(3):
                final_copy(m, number).start()
        for number in (2, 0, 1):
            final_copy(0, number).wait()
            for m in range(1, n_dp):
                final_arrival(m, number).wait_recv()
        total = route_in[0]
        for q in range(1, n_dp):
            total = total + route_in[q]
        lane = lax.broadcasted_iota(jnp.int32, (tok_rows, LANES), 1)
        place = lax.broadcasted_iota(jnp.int32, (tok_rows, top), 1)
        result = jnp.zeros((tok_rows, top), F32)
        for k in range(top):
            col = jnp.sum(jnp.where(lane == ids_ref[:, k : k + 1], total, 0.0), axis=1, keepdims=True)
            result = jnp.where(place == k, col, result)
        route_out[...] = result

    slices()
    first_phase()
    last = len(CHUNKS)
    for t in range(last + 4):
        if 0 <= t - 1 < last:
            stage1(t - 1)
        if t == 1:
            second_phase(3)
            second_phase(2)
        if 0 <= t - 2 < last:
            stage2(t - 2)
        if 0 <= t - 3 < last:
            stage3(t - 3)
        if t == 2:
            for da in (0, 1, 3, 2):
                third_phase(da)
        if t < last:
            take_chunk(t)
            stage0(t)
        if t == 0:
            second_phase(0)
            second_phase(1)
        if 0 <= t - 4 < last:
            stage4(t - 4)
        if 0 <= t - 6 < last:
            fold(t - 6)
    weight_grads()
    for k in range(last - 2, last):
        fold(k)
    finish()

    for m in range(1, n_dp):
        for number in range(3):
            to_slice(m, number).wait_send()
            final_copy(m, number).wait_send()
    for item in sends:
        item.wait_send()
    for k in range(last):
        for way in range(2):
            for number in range(3):
                rs_copy(k, way, number).wait_send()
                ring_copy(k, way, number + 3).wait_send()
        each_back(k, lambda item: item.wait_send())


def moe(tokens, out_grad, ids, weights, gate, up, down, experts, n_dp):
    width, hidden = gate.shape
    tok_rows, top = ids.shape
    slots = min(tok_rows, 3 * tok_rows * top // (2 * experts))
    toks = n_dp * tok_rows
    slots_dp = n_dp * slots
    rows = experts * slots_dp
    quarter = hidden // n_dp
    chunk = GROUP * slots_dp
    both = 2 * width
    last = len(CHUNKS)
    dma = pltpu.SemaphoreType.DMA
    vmem = pltpu.VMEM
    anywhere = pl.BlockSpec(memory_space=pl.ANY)
    inside = pl.BlockSpec(memory_space=pltpu.VMEM)
    return pl.pallas_call(
        moe_kernel,
        out_shape=(
            jax.ShapeDtypeStruct(tokens.shape, BF),
            jax.ShapeDtypeStruct(tokens.shape, BF),
            jax.ShapeDtypeStruct(ids.shape, F32),
            jax.ShapeDtypeStruct((width, hidden), BF),
            jax.ShapeDtypeStruct((width, hidden), BF),
            jax.ShapeDtypeStruct((hidden, width), BF),
            jax.ShapeDtypeStruct((rows, both), BF),
            jax.ShapeDtypeStruct((experts * toks, both + LANES), BF),
        ),
        in_specs=[inside] * 7,
        out_specs=(anywhere, anywhere, inside) + (anywhere,) * 5,
        scratch_shapes=[
            vmem((tok_rows, LANES), BF),
            vmem((toks, both + LANES), BF),
            vmem((GROUP * toks, both + LANES), BF),
            vmem((chunk, width), BF),
            vmem((width, rows), BF),
            vmem((rows, width), BF),
            vmem((hidden, rows), BF),
            vmem((n_dp - 1, 3, rows, quarter), BF),
            vmem((3, rows, quarter), F32),
            vmem((2, 3, rows // 2, quarter), BF),
            vmem((2, 3, rows, quarter), BF),
            vmem((3, rows, hidden), BF),
            vmem((rows, both), BF),
            vmem((2, width, quarter), BF),
            vmem((2, quarter, width), BF),
            vmem((chunk, both), BF),
            vmem((toks, width), F32),
            vmem((toks, width), F32),
            vmem((toks, LANES), F32),
            vmem((toks, both), BF),
            vmem((n_dp, tok_rows, LANES), F32),
            dma((last, 2, 6)),
            dma((last, 2, 6)),
            dma((experts,)),
            dma((experts,)),
            dma((n_dp - 1, 3)),
            dma((n_dp - 1, 3)),
            dma((SIDE * SIDE, 4, 2)),
            dma((SIDE * SIDE, 2)),
            dma((SIDE * SIDE,)),
            dma((SIDE * SIDE,)),
            dma((7,)),
            dma((3, 2)),
            dma((n_dp, 3)),
            dma((n_dp - 1, 3)),
        ],
        compiler_params=pltpu.CompilerParams(
            collective_id=0, has_side_effects=True, vmem_limit_bytes=67043328
        ),
    )(tokens, out_grad, ids, weights, gate, up, down)


def per_device(tokens, ids, weights, out_grad, gate_weight, up_weight, down_weight):
    experts = lax.axis_size("expert")
    n_dp = lax.axis_size("dp")
    mixed, tgrad, route, gate_grad, up_grad, down_grad, _, _ = moe(
        tokens, out_grad, ids, weights, gate_weight[0], up_weight[0], down_weight[0], experts, n_dp
    )
    return (mixed, tgrad, route, gate_grad[None], up_grad[None], down_grad[None])


def solution(mesh):
    rows = P(("dp", "expert"), None)
    weights = (P("expert", "dp", None), P("expert", "dp", None), P("expert", None, "dp"))
    return jax.shard_map(
        per_device,
        mesh=mesh,
        in_specs=(rows, rows, rows, rows) + weights,
        out_specs=(rows, rows, rows) + weights,
        check_vma=False,
    )
```

```python
import jax
import jax.numpy as jnp
from jax import lax
from jax.experimental import pallas as pl
from jax.experimental.pallas import tpu as pltpu
from jax.sharding import PartitionSpec as P

BF = jnp.bfloat16
F32 = jnp.float32
LANES = 128
SIDE = 4
GROUP = 8
CHUNKS = ((0, 4), (8, 8), (24, 8), (16, 8), (4, 4))
MESH = pl.DeviceIdType.MESH


def dot32(a, b, dims, precision=None):
    return lax.dot_general(a, b, (dims, ((), ())), precision=precision, preferred_element_type=F32)


def moe_kernel(
    tok_ref, grad_ref, ids_ref, wts_ref, gate_ref, up_ref, down_ref,
    mixed_out, tgrad_out, route_out, gate_out, up_out, down_out, back_ref, whole_ref,
    square, tab_s, mine, blk, x_s, xt_s, g_s, hid_t, part, own, in_half, in_full, terms, rows_out, stage_a, stage_b,
    bk, mixed_acc, tgrad_acc, route_acc, final_v, route_in,
    ring_send, ring_recv, ret_send, ret_recv, a2a_send, a2a_recv, ag_send, ag_recv,
    pair_send, pair_recv, local_sem, stage_sem, fin_send, fin_recv,
):
    n_dp = lax.axis_size("dp")
    experts = lax.axis_size("expert")
    d = lax.axis_index("dp")
    e = lax.axis_index("expert")
    y = e // (2 * SIDE)
    z = (e // 2) % SIDE
    c = e % 2
    top, tok_rows = ids_ref.shape
    toks = n_dp * tok_rows
    tok_bits = tok_rows.bit_length() - 1
    slots_dp = rows_out.shape[0] // experts
    slots = slots_dp // n_dp
    quarter = own.shape[2]
    width = gate_ref.shape[0]
    to = ((d + n_dp - 1) % n_dp, (d + 1) % n_dp)

    barrier = pltpu.get_barrier_semaphore()
    for m in range(1, n_dp):
        pl.semaphore_signal(barrier, inc=1, device_id={"dp": (d + m) % n_dp}, device_id_type=MESH)

    def greet(step, carry):
        pl.semaphore_signal(
            barrier, inc=1, device_id={"expert": (e + step) % experts}, device_id_type=MESH
        )
        return carry

    lax.fori_loop(1, experts, greet, 0)

    def make_table():
        line = lax.broadcasted_iota(jnp.int32, (LANES, tok_rows), 0)
        name = line & (experts - 1)
        kind = lax.shift_right_logical(line, experts.bit_length() - 1)
        chosen = jnp.zeros((LANES, tok_rows), F32)
        weight = jnp.zeros((LANES, tok_rows), F32)
        for k in range(top):
            same = ids_ref[k : k + 1, :] == name
            chosen += jnp.where(same, 1.0, 0.0)
            weight += jnp.where(same, wts_ref[k : k + 1, :], 0.0)
        row = lax.broadcasted_iota(jnp.int32, (tok_rows, tok_rows), 0)
        col = lax.broadcasted_iota(jnp.int32, (tok_rows, tok_rows), 1)
        before = jnp.where(row <= col, 1.0, 0.0).astype(BF)
        place = jnp.dot(chosen.astype(BF), before, preferred_element_type=F32) * chosen
        high = weight.astype(BF).astype(F32)
        middle = (weight - high).astype(BF).astype(F32)
        low = weight - high - middle
        square[...] = jnp.zeros_like(square)
        square[:, :tok_rows] = jnp.where(
            kind == 0, place, jnp.where(kind == 1, high, jnp.where(kind == 2, middle, low))
        )
        tab_s[...] = square[...].T[:tok_rows].astype(BF)

    make_table()
    pl.semaphore_wait(barrier, experts + n_dp - 2)

    sends = []

    def launch(item):
        item.start()
        sends.append(item)

    def block(p, h=None):
        if h is None:
            return whole_ref.at[pl.ds(p * toks, toks), :]
        rows = toks // 2
        return whole_ref.at[pl.ds(p * toks + h * rows, rows), :]

    def own_slice(src, number):
        rows = pl.ds(pl.multiple_of(src * tok_rows, tok_rows), tok_rows)
        return whole_ref.at[rows, pl.ds(number * width, LANES if number == 2 else width)]

    def to_slice(m, number):
        q = (d + m) % n_dp
        cols = pl.ds(pl.multiple_of(q * width, LANES), width)
        source = tab_s if number == 2 else (tok_ref, grad_ref)[number].at[:, cols]
        target = own_slice(d, number)
        if m == 0:
            return pltpu.make_async_copy(source, target, local_sem.at[number])
        return pltpu.make_async_remote_copy(
            src_ref=source, dst_ref=target, send_sem=a2a_send.at[m - 1, number],
            recv_sem=a2a_recv.at[m - 1, number], device_id={"dp": q}, device_id_type=MESH,
        )

    def from_slice(m, number):
        ref = own_slice((d + n_dp - m) % n_dp, number)
        return pltpu.make_async_remote_copy(
            src_ref=ref, dst_ref=ref, send_sem=a2a_send.at[m - 1, number],
            recv_sem=a2a_recv.at[m - 1, number], device_id={"dp": (d + m) % n_dp}, device_id_type=MESH,
        )

    def spot(da, db, rel):
        return db * GROUP + rel * SIDE + da

    def ag_copy_to(axis, way, da, db, h):
        step = SIDE - 1 if way == 0 else 1
        seen = 1 if way == 0 else SIDE - 1
        da2 = (da + seen) % SIDE if axis == 0 else da
        db2 = (db + seen) % SIDE if axis == 1 else db
        along_y = 1 - c if axis == 0 else c
        y2 = (y + step * along_y) % SIDE
        z2 = (z + step * (1 - along_y)) % SIDE
        return pltpu.make_async_remote_copy(
            src_ref=block(spot(da, db, 0), h),
            dst_ref=block(spot(da2, db2, 0), h),
            send_sem=ag_send.at[da * SIDE + db, axis * 2 + way, h],
            recv_sem=ag_recv.at[da2 * SIDE + db2, h],
            device_id={"expert": (y2 * SIDE + z2) * 2 + c},
            device_id_type=MESH,
        )

    def ag_wait(da, db, h):
        ref = block(spot(da, db, 0), h)
        pltpu.make_async_remote_copy(
            src_ref=ref, dst_ref=ref, send_sem=ag_send.at[0, 0, 0], recv_sem=ag_recv.at[da * SIDE + db, h],
            device_id={"expert": (e + 1) % experts}, device_id_type=MESH,
        ).wait_recv()

    def pair_copy(da, db):
        return pltpu.make_async_remote_copy(
            src_ref=block(spot(da, db, 0)), dst_ref=block(spot(da, db, 1)),
            send_sem=pair_send.at[da * SIDE + db], recv_sem=pair_recv.at[da * SIDE + db],
            device_id={"expert": e + 1 - 2 * c}, device_id_type=MESH,
        )

    def spread(axis, da, db):
        for way, h in ((0, 0), (1, 1), (0, 1), (1, 0)):
            launch(ag_copy_to(axis, way, da, db, h))

    def slices():
        for m in (1, 3, 2, 0):
            for number in range(3):
                to_slice(m, number).start()
        for number in range(3):
            to_slice(0, number).wait()
            for m in range(1, n_dp):
                from_slice(m, number).wait_recv()

    def mine_copy():
        return pltpu.make_async_copy(block(0), mine, local_sem.at[5])

    def first_phase():
        spread(0, 0, 0)
        launch(pair_copy(0, 0))
        mine_copy().start()
        ag_wait(1, 0, 0)
        launch(ag_copy_to(0, 0, 1, 0, 0))
        ag_wait(3, 0, 1)
        launch(ag_copy_to(0, 1, 3, 0, 1))
        spread(1, 0, 0)
        for da in (1, 3):
            ag_wait(da, 0, 1 if da == 1 else 0)
            launch(pair_copy(da, 0))
            spread(1, da, 0)
        ag_wait(2, 0, 0)
        ag_wait(2, 0, 1)
        launch(pair_copy(2, 0))
        spread(1, 2, 0)
        mine_copy().wait()

    def second_phase(da):
        ag_wait(da, 1, 0)
        launch(ag_copy_to(1, 0, da, 1, 0))
        ag_wait(da, 3, 1)
        launch(ag_copy_to(1, 1, da, 3, 1))
        ag_wait(da, 1, 1)
        launch(pair_copy(da, 1))
        ag_wait(da, 3, 0)
        launch(pair_copy(da, 3))

    def third_phase(da):
        ag_wait(da, 2, 0)
        ag_wait(da, 2, 1)
        launch(pair_copy(da, 2))

    def size_of(k):
        return CHUNKS[k][1] * slots_dp

    def rows_of(k, part_half=None):
        start = CHUNKS[k][0] * slots_dp
        if part_half is None:
            return pl.ds(start, size_of(k))
        return pl.ds(start + part_half * (size_of(k) // 2), size_of(k) // 2)

    def half_rows(k):
        return pl.ds(CHUNKS[k][0] * slots_dp // 2, size_of(k) // 2)

    def cols_of(q):
        return pl.ds(pl.multiple_of(q * quarter, quarter), quarter)

    def take_chunk(k):
        first, count = CHUNKS[k]
        for p in range(first, first + count):
            if (p // SIDE) % 2 == 1:
                pair_copy(p % SIDE, p // GROUP).wait_recv()
        load = pltpu.make_async_copy(
            whole_ref.at[pl.ds(first * toks, count * toks), :], blk.at[pl.ds(0, count * toks), :], local_sem.at[3]
        )
        load.start()
        load.wait()
        pair_rows = 2 * slots_dp
        pair_toks = 2 * toks

        def one(i, carry):
            span = pl.ds(pl.multiple_of(i * pair_toks, pair_toks), pair_toks)
            line = lax.broadcasted_iota(jnp.int32, (16, LANES), 0)
            lane = lax.broadcasted_iota(jnp.int32, (16, LANES), 1)
            want = jnp.where((lane == line * experts + e) & (line < 4), 1.0, 0.0).astype(BF)
            found = dot32(want, blk[span, 2 * width :], ((1,), (1,)))
            place = found[0:1, :]
            scale = found[1:2, :] + found[2:3, :] + found[3:4, :]
            token = lax.broadcasted_iota(jnp.int32, (1, pair_toks), 1)
            base = (lax.shift_right_logical(token, tok_bits) * slots).astype(F32)
            goal = jnp.where(place > 0.0, base + place - 1.0, -1.0)
            row = lax.broadcasted_iota(jnp.int32, (pair_rows, pair_toks), 0).astype(F32)
            hit = row == goal
            picked = jnp.dot(
                jnp.where(hit, 1.0, 0.0).astype(BF), blk[span, : 2 * width], preferred_element_type=F32
            )
            scales = jnp.sum(jnp.where(hit, scale, 0.0), axis=1, keepdims=True)
            x_s[pl.ds(pl.multiple_of(i * pair_rows, pair_rows), pair_rows), :] = picked[:, :width].astype(BF)
            g_s[pl.ds(pl.multiple_of(first * slots_dp + i * pair_rows, pair_rows), pair_rows), :] = (
                picked[:, width:] * scales
            ).astype(BF)
            return carry

        lax.fori_loop(0, count // 2, one, 0)

    def copy(k, way, number, source, target):
        return pltpu.make_async_remote_copy(
            src_ref=source, dst_ref=target, send_sem=ring_send.at[k, way, number],
            recv_sem=ring_recv.at[k, way, number], device_id={"dp": to[way]}, device_id_type=MESH,
        )

    def toward(way):
        return part.at[2 if way == 0 else 0]

    def rs_copy(k, way, number):
        if number == 0:
            return copy(k, way, 0, part.at[1, :, rows_of(k, way), :], in_half.at[way, :, half_rows(k), :])
        h = way if number == 2 else 1 - way
        return copy(
            k, way, number, toward(way).at[:, rows_of(k, h), :], in_full.at[way, :, rows_of(k, h), :]
        )

    def ag_terms(k, way, number, q):
        h = way if number in (3, 5) else 1 - way
        ref = terms.at[:, rows_of(k, h), cols_of(q)]
        return copy(k, way, number, ref, ref)

    def ring_copy(k, way, number):
        return ag_terms(k, way, number, to[1 - way] if number == 5 else d)

    def ring_arrival(k, way, number):
        return ag_terms(k, way, number, (d + 2) % n_dp if number == 5 else to[1 - way])

    def partial(k, q, i):
        if i == 2:
            return dot32(g_s[rows_of(k), :], down_ref[cols_of(q), :], ((1,), (1,)))
        right = (gate_ref, up_ref)[i]
        return jnp.dot(x_s[pl.ds(0, size_of(k)), :], right[:, cols_of(q)], preferred_element_type=F32)

    def stage0(k):
        def one(step, carry):
            m = (step + 1) % (n_dp - 1)
            q = (d + m + 1) % n_dp
            for i in range(3):
                part[m, i, rows_of(k), :] = partial(k, q, i).astype(BF)
            return carry

        lax.fori_loop(0, n_dp - 1, one, 0)
        for number in range(2):
            for way in range(2):
                rs_copy(k, way, number).start()
        for i in range(3):
            own[i, rows_of(k), :] = partial(k, d, i)
        xt_s[:, rows_of(k)] = x_s[pl.ds(0, size_of(k)), :].T

    def stage1(k):
        for way in range(2):
            rs_copy(k, way, 0).wait_recv()
            m = 2 if way == 0 else 0
            for i in range(3):
                span = rows_of(k, way)
                total = part[m, i, span, :].astype(F32) + in_half[way, i, half_rows(k), :].astype(F32)
                part[m, i, span, :] = total.astype(BF)
            rs_copy(k, way, 2).start()

    def stage2(k):
        for number in (1, 2):
            for way in range(2):
                rs_copy(k, way, number).wait_recv()

        def total(i, span):
            return own[i, span, :] + in_full[0, i, span, :].astype(F32) + in_full[1, i, span, :].astype(F32)

        step_rows = 2 * slots_dp

        def act(step, carry):
            start = CHUNKS[k][0] * slots_dp + step * step_rows
            span = pl.ds(pl.multiple_of(start, step_rows), step_rows)
            gate = total(0, span)
            up = total(1, span)
            hgrad = total(2, span)
            sig = jax.nn.sigmoid(gate)
            val = gate * sig
            slope = sig * (1.0 + gate * (1.0 - sig))
            terms[0, span, cols_of(d)] = (val * up).astype(BF)
            terms[1, span, cols_of(d)] = (hgrad * up * slope).astype(BF)
            terms[2, span, cols_of(d)] = (hgrad * val).astype(BF)
            return carry

        lax.fori_loop(0, size_of(k) // step_rows, act, 0)
        for number in (3, 4):
            for way in range(2):
                ring_copy(k, way, number).start()

    def stage3(k):
        for way in range(2):
            ring_arrival(k, way, 3).wait_recv()
            ring_copy(k, way, 5).start()

    def home(p):
        return pl.ds(pl.multiple_of(p * slots_dp, slots_dp), slots_dp)

    def back_copy(k, i):
        db = CHUNKS[k][0] // GROUP
        p = CHUNKS[k][0] + i
        s = (c + p // SIDE) % 2
        da = p % SIDE
        y2 = (y + da * (1 - s) + db * s) % SIDE
        z2 = (z + db * (1 - s) + da * s) % SIDE
        return pltpu.make_async_remote_copy(
            src_ref=rows_out.at[home(p), :],
            dst_ref=back_ref.at[home(p), :],
            send_sem=ret_send.at[p],
            recv_sem=ret_recv.at[p],
            device_id={"expert": (y2 * SIDE + z2) * 2 + s},
            device_id_type=MESH,
        )

    def self_copy():
        return pltpu.make_async_copy(rows_out.at[home(0), :], back_ref.at[home(0), :], local_sem.at[4])

    def each_back(k, act):
        def one(i, carry):
            act(back_copy(k, i))
            return carry

        lax.fori_loop(1 if k == 0 else 0, CHUNKS[k][1], one, 0)

    def stage4(k):
        for number in (4, 5):
            for way in range(2):
                ring_arrival(k, way, number).wait_recv()
        half = size_of(k) // 2

        def one(h, carry):
            span = pl.ds(pl.multiple_of(CHUNKS[k][0] * slots_dp + h * half, half), half)
            rows_out[span, :width] = jnp.dot(
                terms[0, span, :], down_ref[...], preferred_element_type=F32
            ).astype(BF)
            rows_out[span, width:] = (
                dot32(terms[1, span, :], gate_ref[...], ((1,), (1,)))
                + dot32(terms[2, span, :], up_ref[...], ((1,), (1,)))
            ).astype(BF)
            return carry

        lax.fori_loop(0, 2, one, 0)
        if k == 0:
            self_copy().start()
        each_back(k, lambda item: item.start())
        hid_t[:, rows_of(k)] = terms[0, rows_of(k), :].T

    def fold(k):
        first, count = CHUNKS[k]
        rows = size_of(k)
        each_back(k, lambda item: item.wait_recv())
        if k == 0:
            self_copy().wait()
        load = pltpu.make_async_copy(back_ref.at[rows_of(k), :], bk.at[pl.ds(0, rows), :], local_sem.at[6])
        load.start()
        row = lax.broadcasted_iota(jnp.int32, (1, rows), 1)
        index = lax.shift_right_logical(row * (65536 // slots_dp + 1), 16)
        local = (row - index * slots_dp).astype(F32)
        p = first + index
        db = first // GROUP
        da = p & (SIDE - 1)
        core = (c + lax.shift_right_logical(p, 2)) & 1
        y2 = (y + 2 * SIDE - (da * (1 - c) + db * c)) & (SIDE - 1)
        z2 = (z + 2 * SIDE - (db * (1 - c) + da * c)) & (SIDE - 1)
        sender = (y2 * SIDE + z2) * 2 + core
        lane = lax.broadcasted_iota(jnp.int32, (LANES, rows), 0)
        names = [jnp.where(lane == kind * experts + sender, 1.0, 0.0) for kind in range(4)]
        table = mine[:, 2 * width :]
        found = [jnp.dot(table, name.astype(BF), preferred_element_type=F32) for name in names]
        token = lax.broadcasted_iota(jnp.int32, (toks, rows), 0)
        base = (lax.shift_right_logical(token, tok_bits) * slots).astype(F32)
        hit = (found[0] > 0.0) & (local == base + found[0] - 1.0)
        scaled = jnp.concatenate([jnp.where(hit, found[i], 0.0).astype(BF) for i in (1, 2, 3)], axis=0)
        once = jnp.where(hit, 1.0, 0.0).astype(BF)
        load.wait()
        outs = bk[pl.ds(0, rows), :width]
        three = jnp.dot(scaled, outs, preferred_element_type=F32)
        mixed = three[:toks] + three[toks : 2 * toks] + three[2 * toks :]
        tgrad = jnp.dot(once, bk[pl.ds(0, rows), width:], preferred_element_type=F32)
        dots = dot32(mine[:, width : 2 * width], outs, ((1,), (1,)))
        route = dot32(jnp.where(hit, dots, 0.0), names[0], ((1,), (1,)), lax.Precision.HIGHEST)
        if k == 0:
            mixed_acc[...] = mixed
            tgrad_acc[...] = tgrad
            route_acc[...] = route
        else:
            mixed_acc[...] += mixed
            tgrad_acc[...] += tgrad
            route_acc[...] += route

    def weight_grads():
        span = stage_a.shape[2]
        tall = stage_b.shape[1]

        def out_copy(kind, i, slot):
            if kind == 2:
                target = down_out.at[pl.ds(pl.multiple_of(i * tall, tall), tall), :]
                return pltpu.make_async_copy(stage_b.at[slot], target, stage_sem.at[kind, slot])
            target = (gate_out, up_out)[kind].at[:, pl.ds(pl.multiple_of(i * span, span), span)]
            return pltpu.make_async_copy(stage_a.at[slot], target, stage_sem.at[kind, slot])

        for kind in range(3):
            count = gate_ref.shape[1] // (tall if kind == 2 else span)

            def one(i, carry, kind=kind):
                slot = i % 2

                @pl.when(i >= 2)
                def _():
                    out_copy(kind, i - 2, slot).wait()

                if kind == 2:
                    left = hid_t[pl.ds(pl.multiple_of(i * tall, tall), tall), :]
                    stage_b[slot] = jnp.dot(left, g_s[...], preferred_element_type=F32).astype(BF)
                else:
                    right = terms[1 + kind, :, pl.ds(pl.multiple_of(i * span, span), span)]
                    stage_a[slot] = jnp.dot(xt_s[...], right, preferred_element_type=F32).astype(BF)
                out_copy(kind, i, slot).start()
                return carry

            lax.fori_loop(0, count, one, 0)
            out_copy(kind, count - 2, count % 2).wait()
            out_copy(kind, count - 1, (count - 1) % 2).wait()

    def final_copy(m, number):
        q = (d + m) % n_dp
        rows = pl.ds(pl.multiple_of(q * tok_rows, tok_rows), tok_rows)
        if number == 2:
            source, target = route_acc.at[rows, :], route_in.at[d]
        else:
            source = final_v.at[rows, pl.ds(number * width, width)]
            target = (mixed_out, tgrad_out)[number].at[:, pl.ds(pl.multiple_of(d * width, LANES), width)]
        if m == 0:
            return pltpu.make_async_copy(source, target, fin_send.at[m, number])
        return pltpu.make_async_remote_copy(
            src_ref=source, dst_ref=target, send_sem=fin_send.at[m, number],
            recv_sem=fin_recv.at[m - 1, number], device_id={"dp": q}, device_id_type=MESH,
        )

    def final_arrival(m, number):
        src = (d + n_dp - m) % n_dp
        if number == 2:
            ref = route_in.at[src]
        else:
            ref = (mixed_out, tgrad_out)[number].at[:, pl.ds(pl.multiple_of(src * width, LANES), width)]
        return pltpu.make_async_remote_copy(
            src_ref=ref, dst_ref=ref, send_sem=fin_send.at[m, number],
            recv_sem=fin_recv.at[m - 1, number], device_id={"dp": (d + m) % n_dp}, device_id_type=MESH,
        )

    def finish():
        final_v[:, :width] = mixed_acc[...].astype(BF)
        final_v[:, width:] = tgrad_acc[...].astype(BF)
        for m in (2, 1, 3, 0):
            for number in range(3):
                final_copy(m, number).start()
        for number in (2, 0, 1):
            final_copy(0, number).wait()
            for m in range(1, n_dp):
                final_arrival(m, number).wait_recv()
        total = route_in[0]
        for q in range(1, n_dp):
            total = total + route_in[q]
        square[:tok_rows, :] = total
        turned = square[...].T[:, :tok_rows]
        line = lax.broadcasted_iota(jnp.int32, (LANES, tok_rows), 0)
        place = lax.broadcasted_iota(jnp.int32, (top, tok_rows), 0)
        result = jnp.zeros((top, tok_rows), F32)
        for k in range(top):
            row = jnp.sum(jnp.where(line == ids_ref[k : k + 1, :], turned, 0.0), axis=0, keepdims=True)
            result = jnp.where(place == k, row, result)
        route_out[...] = result

    slices()
    first_phase()
    last = len(CHUNKS)
    take_chunk(0)
    stage0(0)
    second_phase(0)
    second_phase(1)
    for k in range(last + 1):
        if k < last:
            stage1(k)
        if k >= 1:
            stage3(k - 1)
        if k == 0:
            second_phase(3)
            second_phase(2)
            stage2(0)
        if k + 1 < last:
            take_chunk(k + 1)
            stage0(k + 1)
        if 1 <= k < last:
            stage2(k)
        if k == 1:
            for da in (0, 1, 3, 2):
                third_phase(da)
        if k == last:
            fold(last - 3)
        if k >= 1:
            stage4(k - 1)
        if 2 <= k <= last - 2:
            fold(k - 2)
    weight_grads()
    fold(last - 2)
    fold(last - 1)
    finish()

    for m in range(1, n_dp):
        for number in range(3):
            to_slice(m, number).wait_send()
            final_copy(m, number).wait_send()
    for item in sends:
        item.wait_send()
    for k in range(last):
        for way in range(2):
            for number in range(3):
                rs_copy(k, way, number).wait_send()
                ring_copy(k, way, number + 3).wait_send()
        each_back(k, lambda item: item.wait_send())


def moe(tokens, out_grad, ids, weights, gate, up, down, experts, n_dp):
    width, hidden = gate.shape
    tok_rows, top = ids.shape
    slots = min(tok_rows, 3 * tok_rows * top // (2 * experts))
    toks = n_dp * tok_rows
    slots_dp = n_dp * slots
    rows = experts * slots_dp
    quarter = hidden // n_dp
    chunk = GROUP * slots_dp
    both = 2 * width
    last = len(CHUNKS)
    dma = pltpu.SemaphoreType.DMA
    vmem = pltpu.VMEM
    anywhere = pl.BlockSpec(memory_space=pl.ANY)
    inside = pl.BlockSpec(memory_space=pltpu.VMEM)
    return pl.pallas_call(
        moe_kernel,
        out_shape=(
            jax.ShapeDtypeStruct(tokens.shape, BF),
            jax.ShapeDtypeStruct(tokens.shape, BF),
            jax.ShapeDtypeStruct((top, tok_rows), F32),
            jax.ShapeDtypeStruct((width, hidden), BF),
            jax.ShapeDtypeStruct((width, hidden), BF),
            jax.ShapeDtypeStruct((hidden, width), BF),
            jax.ShapeDtypeStruct((rows, both), BF),
            jax.ShapeDtypeStruct((experts * toks, both + LANES), BF),
        ),
        in_specs=[inside] * 7,
        out_specs=(anywhere, anywhere, inside) + (anywhere,) * 5,
        scratch_shapes=[
            vmem((LANES, LANES), F32),
            vmem((tok_rows, LANES), BF),
            vmem((toks, both + LANES), BF),
            vmem((GROUP * toks, both + LANES), BF),
            vmem((chunk, width), BF),
            vmem((width, rows), BF),
            vmem((rows, width), BF),
            vmem((hidden, rows), BF),
            vmem((n_dp - 1, 3, rows, quarter), BF),
            vmem((3, rows, quarter), F32),
            vmem((2, 3, rows // 2, quarter), BF),
            vmem((2, 3, rows, quarter), BF),
            vmem((3, rows, hidden), BF),
            vmem((rows, both), BF),
            vmem((2, width, quarter), BF),
            vmem((2, quarter, width), BF),
            vmem((chunk, both), BF),
            vmem((toks, width), F32),
            vmem((toks, width), F32),
            vmem((toks, LANES), F32),
            vmem((toks, both), BF),
            vmem((n_dp, tok_rows, LANES), F32),
            dma((last, 2, 6)),
            dma((last, 2, 6)),
            dma((experts,)),
            dma((experts,)),
            dma((n_dp - 1, 3)),
            dma((n_dp - 1, 3)),
            dma((SIDE * SIDE, 4, 2)),
            dma((SIDE * SIDE, 2)),
            dma((SIDE * SIDE,)),
            dma((SIDE * SIDE,)),
            dma((7,)),
            dma((3, 2)),
            dma((n_dp, 3)),
            dma((n_dp - 1, 3)),
        ],
        compiler_params=pltpu.CompilerParams(
            collective_id=0, has_side_effects=True, vmem_limit_bytes=67043328
        ),
    )(tokens, out_grad, ids.T, weights.T, gate, up, down)


def per_device(tokens, ids, weights, out_grad, gate_weight, up_weight, down_weight):
    experts = lax.axis_size("expert")
    n_dp = lax.axis_size("dp")
    mixed, tgrad, route, gate_grad, up_grad, down_grad, _, _ = moe(
        tokens, out_grad, ids, weights, gate_weight[0], up_weight[0], down_weight[0], experts, n_dp
    )
    return (mixed, tgrad, route.T, gate_grad[None], up_grad[None], down_grad[None])


def solution(mesh):
    rows = P(("dp", "expert"), None)
    weights = (P("expert", "dp", None), P("expert", "dp", None), P("expert", None, "dp"))
    return jax.shard_map(
        per_device,
        mesh=mesh,
        in_specs=(rows, rows, rows, rows) + weights,
        out_specs=(rows, rows, rows) + weights,
        check_vma=False,
    )
```

```python
import jax
import jax.numpy as jnp
from jax import lax
from jax.experimental import pallas as pl
from jax.experimental.pallas import tpu as pltpu
from jax.sharding import PartitionSpec as P

BF = jnp.bfloat16
F32 = jnp.float32
LANES = 128
SIDE = 4
GROUP = 8
CHUNKS = ((0, 2), (2, 6), (8, 8), (16, 8), (24, 4), (28, 4))
MESH = pl.DeviceIdType.MESH


def dot32(a, b, dims, precision=None):
    return lax.dot_general(a, b, (dims, ((), ())), precision=precision, preferred_element_type=F32)


def moe_kernel(
    tok_ref, grad_ref, ids_ref, wts_ref, gate_hbm, up_hbm, down_hbm,
    mixed_out, tgrad_out, route_out, gate_out, up_out, down_out, back_ref, whole_ref,
    gate_ref, up_ref, down_ref, square, tab_s, mine, blk, x_s, xt_s, g_s, hid_t, part, own, in_half, in_full, terms, rows_out, stage_a, stage_b,
    bk, mixed_acc, tgrad_acc, route_acc, final_v, route_in,
    ring_send, ring_recv, ret_send, ret_recv, a2a_send, a2a_recv, ag_send, ag_recv,
    pair_send, pair_recv, local_sem, stage_sem, fin_send, fin_recv,
):
    n_dp = lax.axis_size("dp")
    experts = lax.axis_size("expert")
    d = lax.axis_index("dp")
    e = lax.axis_index("expert")
    y = e // (2 * SIDE)
    z = (e // 2) % SIDE
    c = e % 2
    top, tok_rows = ids_ref.shape
    toks = n_dp * tok_rows
    tok_bits = tok_rows.bit_length() - 1
    slots_dp = rows_out.shape[0] // experts
    slots = slots_dp // n_dp
    quarter = own.shape[2]
    width = gate_ref.shape[0]
    to = ((d + n_dp - 1) % n_dp, (d + 1) % n_dp)

    barrier = pltpu.get_barrier_semaphore()
    for m in range(1, n_dp):
        pl.semaphore_signal(barrier, inc=1, device_id={"dp": (d + m) % n_dp}, device_id_type=MESH)

    loads = [
        pltpu.make_async_copy(source, target, local_sem.at[7 + i])
        for i, (source, target) in enumerate(((gate_hbm, gate_ref), (up_hbm, up_ref), (down_hbm, down_ref)))
    ]
    for item in loads:
        item.start()

    def greet(step, carry):
        pl.semaphore_signal(
            barrier, inc=1, device_id={"expert": (e + step) % experts}, device_id_type=MESH
        )
        return carry

    lax.fori_loop(1, experts, greet, 0)

    def make_table():
        line = lax.broadcasted_iota(jnp.int32, (LANES, tok_rows), 0)
        name = line & (experts - 1)
        kind = lax.shift_right_logical(line, experts.bit_length() - 1)
        chosen = jnp.zeros((LANES, tok_rows), F32)
        weight = jnp.zeros((LANES, tok_rows), F32)
        for k in range(top):
            same = ids_ref[k : k + 1, :] == name
            chosen += jnp.where(same, 1.0, 0.0)
            weight += jnp.where(same, wts_ref[k : k + 1, :], 0.0)
        row = lax.broadcasted_iota(jnp.int32, (tok_rows, tok_rows), 0)
        col = lax.broadcasted_iota(jnp.int32, (tok_rows, tok_rows), 1)
        before = jnp.where(row <= col, 1.0, 0.0).astype(BF)
        place = jnp.dot(chosen.astype(BF), before, preferred_element_type=F32) * chosen
        high = weight.astype(BF).astype(F32)
        middle = (weight - high).astype(BF).astype(F32)
        low = weight - high - middle
        square[...] = jnp.zeros_like(square)
        square[:, :tok_rows] = jnp.where(
            kind == 0, place, jnp.where(kind == 1, high, jnp.where(kind == 2, middle, low))
        )
        tab_s[...] = square[...].T[:tok_rows].astype(BF)

    make_table()
    pl.semaphore_wait(barrier, experts + n_dp - 2)

    sends = []

    def launch(item):
        item.start()
        sends.append(item)

    def block(p, h=None):
        if h is None:
            return whole_ref.at[pl.ds(p * toks, toks), :]
        rows = toks // 2
        return whole_ref.at[pl.ds(p * toks + h * rows, rows), :]

    def own_slice(src, number):
        rows = pl.ds(pl.multiple_of(src * tok_rows, tok_rows), tok_rows)
        return whole_ref.at[rows, pl.ds(number * width, LANES if number == 2 else width)]

    def to_slice(m, number):
        q = (d + m) % n_dp
        cols = pl.ds(pl.multiple_of(q * width, LANES), width)
        source = tab_s if number == 2 else (tok_ref, grad_ref)[number].at[:, cols]
        target = own_slice(d, number)
        if m == 0:
            return pltpu.make_async_copy(source, target, local_sem.at[number])
        return pltpu.make_async_remote_copy(
            src_ref=source, dst_ref=target, send_sem=a2a_send.at[m - 1, number],
            recv_sem=a2a_recv.at[m - 1, number], device_id={"dp": q}, device_id_type=MESH,
        )

    def from_slice(m, number):
        ref = own_slice((d + n_dp - m) % n_dp, number)
        return pltpu.make_async_remote_copy(
            src_ref=ref, dst_ref=ref, send_sem=a2a_send.at[m - 1, number],
            recv_sem=a2a_recv.at[m - 1, number], device_id={"dp": (d + m) % n_dp}, device_id_type=MESH,
        )

    def spot(da, db, rel):
        return db * GROUP + da * 2 + rel

    def ag_copy_to(axis, way, da, db, h):
        step = SIDE - 1 if way == 0 else 1
        seen = 1 if way == 0 else SIDE - 1
        da2 = (da + seen) % SIDE if axis == 0 else da
        db2 = (db + seen) % SIDE if axis == 1 else db
        along_y = 1 - c if axis == 0 else c
        y2 = (y + step * along_y) % SIDE
        z2 = (z + step * (1 - along_y)) % SIDE
        return pltpu.make_async_remote_copy(
            src_ref=block(spot(da, db, 0), h),
            dst_ref=block(spot(da2, db2, 0), h),
            send_sem=ag_send.at[da * SIDE + db, axis * 2 + way, h],
            recv_sem=ag_recv.at[da2 * SIDE + db2, h],
            device_id={"expert": (y2 * SIDE + z2) * 2 + c},
            device_id_type=MESH,
        )

    def ag_wait(da, db, h):
        ref = block(spot(da, db, 0), h)
        pltpu.make_async_remote_copy(
            src_ref=ref, dst_ref=ref, send_sem=ag_send.at[0, 0, 0], recv_sem=ag_recv.at[da * SIDE + db, h],
            device_id={"expert": (e + 1) % experts}, device_id_type=MESH,
        ).wait_recv()

    def pair_copy(da, db):
        return pltpu.make_async_remote_copy(
            src_ref=block(spot(da, db, 0)), dst_ref=block(spot(da, db, 1)),
            send_sem=pair_send.at[da * SIDE + db], recv_sem=pair_recv.at[da * SIDE + db],
            device_id={"expert": e + 1 - 2 * c}, device_id_type=MESH,
        )

    def spread(axis, da, db):
        for way, h in ((0, 0), (1, 1), (0, 1), (1, 0)):
            launch(ag_copy_to(axis, way, da, db, h))

    def slices():
        for m in (1, 3, 2, 0):
            for number in range(3):
                to_slice(m, number).start()
        for number in range(3):
            to_slice(0, number).wait()
            for m in range(1, n_dp):
                from_slice(m, number).wait_recv()

    def mine_copy():
        return pltpu.make_async_copy(block(0), mine, local_sem.at[5])

    def own_phase():
        launch(pair_copy(0, 0))
        spread(0, 0, 0)
        mine_copy().start()

    def first_phase():
        ag_wait(1, 0, 0)
        launch(ag_copy_to(0, 0, 1, 0, 0))
        ag_wait(3, 0, 1)
        launch(ag_copy_to(0, 1, 3, 0, 1))
        spread(1, 0, 0)
        for da in (1, 3):
            ag_wait(da, 0, 1 if da == 1 else 0)
            launch(pair_copy(da, 0))
            spread(1, da, 0)
        ag_wait(2, 0, 0)
        ag_wait(2, 0, 1)
        launch(pair_copy(2, 0))
        spread(1, 2, 0)
        mine_copy().wait()

    def second_phase(da):
        ag_wait(da, 1, 0)
        launch(ag_copy_to(1, 0, da, 1, 0))
        ag_wait(da, 3, 1)
        launch(ag_copy_to(1, 1, da, 3, 1))
        ag_wait(da, 1, 1)
        launch(pair_copy(da, 1))
        ag_wait(da, 3, 0)
        launch(pair_copy(da, 3))

    def third_phase(da):
        ag_wait(da, 2, 0)
        ag_wait(da, 2, 1)
        launch(pair_copy(da, 2))

    def size_of(k):
        return CHUNKS[k][1] * slots_dp

    def rows_of(k, part_half=None):
        start = CHUNKS[k][0] * slots_dp
        if part_half is None:
            return pl.ds(start, size_of(k))
        return pl.ds(start + part_half * (size_of(k) // 2), size_of(k) // 2)

    def half_rows(k):
        return pl.ds(CHUNKS[k][0] * slots_dp // 2, size_of(k) // 2)

    def cols_of(q):
        return pl.ds(pl.multiple_of(q * quarter, quarter), quarter)

    def take_chunk(k):
        first, count = CHUNKS[k]
        for p in range(first, first + count):
            if p % 2 == 1:
                pair_copy((p // 2) % SIDE, p // GROUP).wait_recv()
        load = pltpu.make_async_copy(
            whole_ref.at[pl.ds(first * toks, count * toks), :], blk.at[pl.ds(0, count * toks), :], local_sem.at[3]
        )
        load.start()
        load.wait()
        pair_rows = 2 * slots_dp
        pair_toks = 2 * toks

        def one(i, carry):
            span = pl.ds(pl.multiple_of(i * pair_toks, pair_toks), pair_toks)
            line = lax.broadcasted_iota(jnp.int32, (16, LANES), 0)
            lane = lax.broadcasted_iota(jnp.int32, (16, LANES), 1)
            want = jnp.where((lane == line * experts + e) & (line < 4), 1.0, 0.0).astype(BF)
            found = dot32(want, blk[span, 2 * width :], ((1,), (1,)))
            place = found[0:1, :]
            scale = found[1:2, :] + found[2:3, :] + found[3:4, :]
            token = lax.broadcasted_iota(jnp.int32, (1, pair_toks), 1)
            base = (lax.shift_right_logical(token, tok_bits) * slots).astype(F32)
            goal = jnp.where(place > 0.0, base + place - 1.0, -1.0)
            row = lax.broadcasted_iota(jnp.int32, (pair_rows, pair_toks), 0).astype(F32)
            hit = row == goal
            picked = jnp.dot(
                jnp.where(hit, 1.0, 0.0).astype(BF), blk[span, : 2 * width], preferred_element_type=F32
            )
            scales = jnp.sum(jnp.where(hit, scale, 0.0), axis=1, keepdims=True)
            x_s[pl.ds(pl.multiple_of(i * pair_rows, pair_rows), pair_rows), :] = picked[:, :width].astype(BF)
            g_s[pl.ds(pl.multiple_of(first * slots_dp + i * pair_rows, pair_rows), pair_rows), :] = (
                picked[:, width:] * scales
            ).astype(BF)
            return carry

        lax.fori_loop(0, count // 2, one, 0)

    def copy(k, way, number, source, target):
        return pltpu.make_async_remote_copy(
            src_ref=source, dst_ref=target, send_sem=ring_send.at[k, way, number],
            recv_sem=ring_recv.at[k, way, number], device_id={"dp": to[way]}, device_id_type=MESH,
        )

    def toward(way):
        return part.at[2 if way == 0 else 0]

    def rs_copy(k, way, number):
        if number == 0:
            return copy(k, way, 0, part.at[1, :, rows_of(k, way), :], in_half.at[way, :, half_rows(k), :])
        h = way if number == 2 else 1 - way
        return copy(
            k, way, number, toward(way).at[:, rows_of(k, h), :], in_full.at[way, :, rows_of(k, h), :]
        )

    def ag_terms(k, way, number, q):
        h = way if number in (3, 5) else 1 - way
        ref = terms.at[:, rows_of(k, h), cols_of(q)]
        return copy(k, way, number, ref, ref)

    def ring_copy(k, way, number):
        return ag_terms(k, way, number, to[1 - way] if number == 5 else d)

    def ring_arrival(k, way, number):
        return ag_terms(k, way, number, (d + 2) % n_dp if number == 5 else to[1 - way])

    def partial(k, q, i):
        if i == 2:
            return dot32(g_s[rows_of(k), :], down_ref[cols_of(q), :], ((1,), (1,)))
        right = (gate_ref, up_ref)[i]
        return jnp.dot(x_s[pl.ds(0, size_of(k)), :], right[:, cols_of(q)], preferred_element_type=F32)

    def stage0(k):
        def one(step, carry):
            m = (step + 1) % (n_dp - 1)
            q = (d + m + 1) % n_dp
            for i in range(3):
                part[m, i, rows_of(k), :] = partial(k, q, i).astype(BF)
            return carry

        lax.fori_loop(0, n_dp - 1, one, 0)
        for number in range(2):
            for way in range(2):
                rs_copy(k, way, number).start()
        for i in range(3):
            own[i, rows_of(k), :] = partial(k, d, i)
        xt_s[:, rows_of(k)] = x_s[pl.ds(0, size_of(k)), :].T

    def stage1(k):
        for way in range(2):
            rs_copy(k, way, 0).wait_recv()
            m = 2 if way == 0 else 0
            for i in range(3):
                span = rows_of(k, way)
                total = part[m, i, span, :].astype(F32) + in_half[way, i, half_rows(k), :].astype(F32)
                part[m, i, span, :] = total.astype(BF)
            rs_copy(k, way, 2).start()

    def stage2(k):
        for number in (1, 2):
            for way in range(2):
                rs_copy(k, way, number).wait_recv()

        def total(i, span):
            return own[i, span, :] + in_full[0, i, span, :].astype(F32) + in_full[1, i, span, :].astype(F32)

        step_rows = 2 * slots_dp

        def act(step, carry):
            start = CHUNKS[k][0] * slots_dp + step * step_rows
            span = pl.ds(pl.multiple_of(start, step_rows), step_rows)
            gate = total(0, span)
            up = total(1, span)
            hgrad = total(2, span)
            sig = jax.nn.sigmoid(gate)
            val = gate * sig
            slope = sig * (1.0 + gate * (1.0 - sig))
            terms[0, span, cols_of(d)] = (val * up).astype(BF)
            terms[1, span, cols_of(d)] = (hgrad * up * slope).astype(BF)
            terms[2, span, cols_of(d)] = (hgrad * val).astype(BF)
            return carry

        lax.fori_loop(0, size_of(k) // step_rows, act, 0)
        for number in (3, 4):
            for way in range(2):
                ring_copy(k, way, number).start()

    def stage3(k):
        for way in range(2):
            ring_arrival(k, way, 3).wait_recv()
            ring_copy(k, way, 5).start()

    def home(p):
        return pl.ds(pl.multiple_of(p * slots_dp, slots_dp), slots_dp)

    def back_copy(k, i):
        db = CHUNKS[k][0] // GROUP
        p = CHUNKS[k][0] + i
        s = (c + p) % 2
        da = (p // 2) % SIDE
        y2 = (y + da * (1 - s) + db * s) % SIDE
        z2 = (z + db * (1 - s) + da * s) % SIDE
        return pltpu.make_async_remote_copy(
            src_ref=rows_out.at[home(p), :],
            dst_ref=back_ref.at[home(p), :],
            send_sem=ret_send.at[p],
            recv_sem=ret_recv.at[p],
            device_id={"expert": (y2 * SIDE + z2) * 2 + s},
            device_id_type=MESH,
        )

    def self_copy():
        return pltpu.make_async_copy(rows_out.at[home(0), :], back_ref.at[home(0), :], local_sem.at[4])

    def each_back(k, act):
        def one(i, carry):
            act(back_copy(k, i))
            return carry

        lax.fori_loop(1 if k == 0 else 0, CHUNKS[k][1], one, 0)

    def stage4(k):
        for number in (4, 5):
            for way in range(2):
                ring_arrival(k, way, number).wait_recv()
        half = size_of(k) // 2

        def one(h, carry):
            span = pl.ds(pl.multiple_of(CHUNKS[k][0] * slots_dp + h * half, slots_dp), half)
            rows_out[span, :width] = jnp.dot(
                terms[0, span, :], down_ref[...], preferred_element_type=F32
            ).astype(BF)
            rows_out[span, width:] = (
                dot32(terms[1, span, :], gate_ref[...], ((1,), (1,)))
                + dot32(terms[2, span, :], up_ref[...], ((1,), (1,)))
            ).astype(BF)
            return carry

        lax.fori_loop(0, 2, one, 0)
        if k == 0:
            self_copy().start()
        each_back(k, lambda item: item.start())
        hid_t[:, rows_of(k)] = terms[0, rows_of(k), :].T

    def fold(k):
        first, count = CHUNKS[k]
        rows = size_of(k)
        each_back(k, lambda item: item.wait_recv())
        if k == 0:
            self_copy().wait()
        load = pltpu.make_async_copy(back_ref.at[rows_of(k), :], bk.at[pl.ds(0, rows), :], local_sem.at[6])
        load.start()
        row = lax.broadcasted_iota(jnp.int32, (1, rows), 1)
        index = lax.shift_right_logical(row * (65536 // slots_dp + 1), 16)
        local = (row - index * slots_dp).astype(F32)
        p = first + index
        db = first // GROUP
        da = lax.shift_right_logical(p, 1) & (SIDE - 1)
        core = (c + p) & 1
        y2 = (y + 2 * SIDE - (da * (1 - c) + db * c)) & (SIDE - 1)
        z2 = (z + 2 * SIDE - (db * (1 - c) + da * c)) & (SIDE - 1)
        sender = (y2 * SIDE + z2) * 2 + core
        lane = lax.broadcasted_iota(jnp.int32, (LANES, rows), 0)
        names = [jnp.where(lane == kind * experts + sender, 1.0, 0.0) for kind in range(4)]
        table = mine[:, 2 * width :]
        found = [jnp.dot(table, name.astype(BF), preferred_element_type=F32) for name in names]
        token = lax.broadcasted_iota(jnp.int32, (toks, rows), 0)
        base = (lax.shift_right_logical(token, tok_bits) * slots).astype(F32)
        hit = (found[0] > 0.0) & (local == base + found[0] - 1.0)
        scaled = jnp.concatenate([jnp.where(hit, found[i], 0.0).astype(BF) for i in (1, 2, 3)], axis=0)
        once = jnp.where(hit, 1.0, 0.0).astype(BF)
        load.wait()
        outs = bk[pl.ds(0, rows), :width]
        three = jnp.dot(scaled, outs, preferred_element_type=F32)
        mixed = three[:toks] + three[toks : 2 * toks] + three[2 * toks :]
        tgrad = jnp.dot(once, bk[pl.ds(0, rows), width:], preferred_element_type=F32)
        dots = dot32(mine[:, width : 2 * width], outs, ((1,), (1,)))
        route = dot32(jnp.where(hit, dots, 0.0), names[0], ((1,), (1,)), lax.Precision.HIGHEST)
        if k == 0:
            mixed_acc[...] = mixed
            tgrad_acc[...] = tgrad
            route_acc[...] = route
        else:
            mixed_acc[...] += mixed
            tgrad_acc[...] += tgrad
            route_acc[...] += route

    def weight_grads():
        span = stage_a.shape[2]
        tall = stage_b.shape[1]

        def out_copy(kind, i, slot):
            if kind == 2:
                target = down_out.at[pl.ds(pl.multiple_of(i * tall, tall), tall), :]
                return pltpu.make_async_copy(stage_b.at[slot], target, stage_sem.at[kind, slot])
            target = (gate_out, up_out)[kind].at[:, pl.ds(pl.multiple_of(i * span, span), span)]
            return pltpu.make_async_copy(stage_a.at[slot], target, stage_sem.at[kind, slot])

        for kind in range(3):
            count = gate_ref.shape[1] // (tall if kind == 2 else span)

            def one(i, carry, kind=kind):
                slot = i % 2

                @pl.when(i >= 2)
                def _():
                    out_copy(kind, i - 2, slot).wait()

                if kind == 2:
                    left = hid_t[pl.ds(pl.multiple_of(i * tall, tall), tall), :]
                    stage_b[slot] = jnp.dot(left, g_s[...], preferred_element_type=F32).astype(BF)
                else:
                    right = terms[1 + kind, :, pl.ds(pl.multiple_of(i * span, span), span)]
                    stage_a[slot] = jnp.dot(xt_s[...], right, preferred_element_type=F32).astype(BF)
                out_copy(kind, i, slot).start()
                return carry

            lax.fori_loop(0, count, one, 0)
            out_copy(kind, count - 2, count % 2).wait()
            out_copy(kind, count - 1, (count - 1) % 2).wait()

    def final_copy(m, number):
        q = (d + m) % n_dp
        rows = pl.ds(pl.multiple_of(q * tok_rows, tok_rows), tok_rows)
        if number == 2:
            source, target = route_acc.at[rows, :], route_in.at[d]
        else:
            source = final_v.at[rows, pl.ds(number * width, width)]
            target = (mixed_out, tgrad_out)[number].at[:, pl.ds(pl.multiple_of(d * width, LANES), width)]
        if m == 0:
            return pltpu.make_async_copy(source, target, fin_send.at[m, number])
        return pltpu.make_async_remote_copy(
            src_ref=source, dst_ref=target, send_sem=fin_send.at[m, number],
            recv_sem=fin_recv.at[m - 1, number], device_id={"dp": q}, device_id_type=MESH,
        )

    def final_arrival(m, number):
        src = (d + n_dp - m) % n_dp
        if number == 2:
            ref = route_in.at[src]
        else:
            ref = (mixed_out, tgrad_out)[number].at[:, pl.ds(pl.multiple_of(src * width, LANES), width)]
        return pltpu.make_async_remote_copy(
            src_ref=ref, dst_ref=ref, send_sem=fin_send.at[m, number],
            recv_sem=fin_recv.at[m - 1, number], device_id={"dp": (d + m) % n_dp}, device_id_type=MESH,
        )

    def finish():
        final_v[:, :width] = mixed_acc[...].astype(BF)
        final_v[:, width:] = tgrad_acc[...].astype(BF)
        for m in (2, 1, 3, 0):
            for number in range(3):
                final_copy(m, number).start()
        for number in (2, 0, 1):
            final_copy(0, number).wait()
            for m in range(1, n_dp):
                final_arrival(m, number).wait_recv()
        total = route_in[0]
        for q in range(1, n_dp):
            total = total + route_in[q]
        square[:tok_rows, :] = total
        turned = square[...].T[:, :tok_rows]
        line = lax.broadcasted_iota(jnp.int32, (LANES, tok_rows), 0)
        place = lax.broadcasted_iota(jnp.int32, (top, tok_rows), 0)
        result = jnp.zeros((top, tok_rows), F32)
        for k in range(top):
            row = jnp.sum(jnp.where(line == ids_ref[k : k + 1, :], turned, 0.0), axis=0, keepdims=True)
            result = jnp.where(place == k, row, result)
        route_out[...] = result

    slices()
    own_phase()
    last = len(CHUNKS)
    for item in loads:
        item.wait()
    take_chunk(0)
    stage0(0)
    first_phase()
    for k in range(last + 1):
        if k < last:
            stage1(k)
        if k >= 1:
            stage3(k - 1)
        if k + 1 < last:
            take_chunk(k + 1)
            stage0(k + 1)
        if k == 0:
            second_phase(0)
            second_phase(1)
            stage2(0)
            second_phase(3)
            second_phase(2)
        if 1 <= k < last:
            stage2(k)
        if k == 1:
            for da in (0, 1, 3, 2):
                third_phase(da)
        if k >= 1:
            stage4(k - 1)
        if 2 <= k <= last - 2:
            fold(k - 2)
    weight_grads()
    fold(last - 3)
    fold(last - 2)
    fold(last - 1)
    finish()

    for m in range(1, n_dp):
        for number in range(3):
            to_slice(m, number).wait_send()
            final_copy(m, number).wait_send()
    for item in sends:
        item.wait_send()
    for k in range(last):
        for way in range(2):
            for number in range(3):
                rs_copy(k, way, number).wait_send()
                ring_copy(k, way, number + 3).wait_send()
        each_back(k, lambda item: item.wait_send())


def moe(tokens, out_grad, ids, weights, gate, up, down, experts, n_dp):
    width, hidden = gate.shape
    tok_rows, top = ids.shape
    slots = min(tok_rows, 3 * tok_rows * top // (2 * experts))
    toks = n_dp * tok_rows
    slots_dp = n_dp * slots
    rows = experts * slots_dp
    quarter = hidden // n_dp
    chunk = GROUP * slots_dp
    both = 2 * width
    last = len(CHUNKS)
    dma = pltpu.SemaphoreType.DMA
    vmem = pltpu.VMEM
    anywhere = pl.BlockSpec(memory_space=pl.ANY)
    inside = pl.BlockSpec(memory_space=pltpu.VMEM)
    return pl.pallas_call(
        moe_kernel,
        out_shape=(
            jax.ShapeDtypeStruct(tokens.shape, BF),
            jax.ShapeDtypeStruct(tokens.shape, BF),
            jax.ShapeDtypeStruct((top, tok_rows), F32),
            jax.ShapeDtypeStruct((width, hidden), BF),
            jax.ShapeDtypeStruct((width, hidden), BF),
            jax.ShapeDtypeStruct((hidden, width), BF),
            jax.ShapeDtypeStruct((rows, both), BF),
            jax.ShapeDtypeStruct((experts * toks, both + LANES), BF),
        ),
        in_specs=[anywhere, anywhere, inside, inside, anywhere, anywhere, anywhere],
        out_specs=(anywhere, anywhere, inside) + (anywhere,) * 5,
        scratch_shapes=[
            vmem((width, hidden), BF),
            vmem((width, hidden), BF),
            vmem((hidden, width), BF),
            vmem((LANES, LANES), F32),
            vmem((tok_rows, LANES), BF),
            vmem((toks, both + LANES), BF),
            vmem((GROUP * toks, both + LANES), BF),
            vmem((chunk, width), BF),
            vmem((width, rows), BF),
            vmem((rows, width), BF),
            vmem((hidden, rows), BF),
            vmem((n_dp - 1, 3, rows, quarter), BF),
            vmem((3, rows, quarter), F32),
            vmem((2, 3, rows // 2, quarter), BF),
            vmem((2, 3, rows, quarter), BF),
            vmem((3, rows, hidden), BF),
            vmem((rows, both), BF),
            vmem((2, width, quarter), BF),
            vmem((2, quarter, width), BF),
            vmem((chunk, both), BF),
            vmem((toks, width), F32),
            vmem((toks, width), F32),
            vmem((toks, LANES), F32),
            vmem((toks, both), BF),
            vmem((n_dp, tok_rows, LANES), F32),
            dma((last, 2, 6)),
            dma((last, 2, 6)),
            dma((experts,)),
            dma((experts,)),
            dma((n_dp - 1, 3)),
            dma((n_dp - 1, 3)),
            dma((SIDE * SIDE, 4, 2)),
            dma((SIDE * SIDE, 2)),
            dma((SIDE * SIDE,)),
            dma((SIDE * SIDE,)),
            dma((10,)),
            dma((3, 2)),
            dma((n_dp, 3)),
            dma((n_dp - 1, 3)),
        ],
        compiler_params=pltpu.CompilerParams(
            collective_id=0, has_side_effects=True, vmem_limit_bytes=67043328
        ),
    )(tokens, out_grad, ids.T, weights.T, gate, up, down)


def per_device(tokens, ids, weights, out_grad, gate_weight, up_weight, down_weight):
    experts = lax.axis_size("expert")
    n_dp = lax.axis_size("dp")
    mixed, tgrad, route, gate_grad, up_grad, down_grad, _, _ = moe(
        tokens, out_grad, ids, weights, gate_weight[0], up_weight[0], down_weight[0], experts, n_dp
    )
    return (mixed, tgrad, route.T, gate_grad[None], up_grad[None], down_grad[None])


def solution(mesh):
    rows = P(("dp", "expert"), None)
    weights = (P("expert", "dp", None), P("expert", "dp", None), P("expert", None, "dp"))
    return jax.shard_map(
        per_device,
        mesh=mesh,
        in_specs=(rows, rows, rows, rows) + weights,
        out_specs=(rows, rows, rows) + weights,
        check_vma=False,
    )
```

```python
import jax
import jax.numpy as jnp
from jax import lax
from jax.experimental import pallas as pl
from jax.experimental.pallas import tpu as pltpu
from jax.sharding import PartitionSpec as P

BF = jnp.bfloat16
F32 = jnp.float32
LANES = 128
SIDE = 4
GROUP = 8
CHUNKS = ((0, 2), (2, 2), (8, 8), (16, 8), (24, 4), (28, 4), (4, 4))
MESH = pl.DeviceIdType.MESH


def dot32(a, b, dims, precision=None):
    return lax.dot_general(a, b, (dims, ((), ())), precision=precision, preferred_element_type=F32)


def moe_kernel(
    tok_ref, grad_ref, ids_ref, wts_ref, gate_hbm, up_hbm, down_hbm,
    mixed_out, tgrad_out, route_out, gate_out, up_out, down_out, back_ref, whole_ref,
    gate_ref, up_ref, down_ref, square, tab_s, mine, blk, x_s, xt_s, g_s, hid_t, part, own, in_half, in_full, terms, rows_out, stage_a, stage_b,
    bk, mixed_acc, tgrad_acc, route_acc, final_v, route_in,
    ring_send, ring_recv, ret_send, ret_recv, a2a_send, a2a_recv, ag_send, ag_recv,
    pair_send, pair_recv, local_sem, stage_sem, fin_send, fin_recv,
):
    n_dp = lax.axis_size("dp")
    experts = lax.axis_size("expert")
    d = lax.axis_index("dp")
    e = lax.axis_index("expert")
    y = e // (2 * SIDE)
    z = (e // 2) % SIDE
    c = e % 2
    top, tok_rows = ids_ref.shape
    toks = n_dp * tok_rows
    tok_bits = tok_rows.bit_length() - 1
    slots_dp = rows_out.shape[0] // experts
    slots = slots_dp // n_dp
    quarter = own.shape[2]
    width = gate_ref.shape[0]
    to = ((d + n_dp - 1) % n_dp, (d + 1) % n_dp)

    barrier = pltpu.get_barrier_semaphore()
    for m in range(1, n_dp):
        pl.semaphore_signal(barrier, inc=1, device_id={"dp": (d + m) % n_dp}, device_id_type=MESH)

    loads = [
        pltpu.make_async_copy(source, target, local_sem.at[7 + i])
        for i, (source, target) in enumerate(((gate_hbm, gate_ref), (up_hbm, up_ref), (down_hbm, down_ref)))
    ]
    for item in loads:
        item.start()

    near = [e + 1 - 2 * c]
    for step in (1, SIDE - 1):
        near.append((((y + step) % SIDE) * SIDE + z) * 2 + c)
        near.append((y * SIDE + (z + step) % SIDE) * 2 + c)
    for peer in near:
        pl.semaphore_signal(barrier, inc=1, device_id={"expert": peer}, device_id_type=MESH)

    def make_table():
        line = lax.broadcasted_iota(jnp.int32, (LANES, tok_rows), 0)
        name = line & (experts - 1)
        kind = lax.shift_right_logical(line, experts.bit_length() - 1)
        chosen = jnp.zeros((LANES, tok_rows), F32)
        weight = jnp.zeros((LANES, tok_rows), F32)
        for k in range(top):
            same = ids_ref[k : k + 1, :] == name
            chosen += jnp.where(same, 1.0, 0.0)
            weight += jnp.where(same, wts_ref[k : k + 1, :], 0.0)
        row = lax.broadcasted_iota(jnp.int32, (tok_rows, tok_rows), 0)
        col = lax.broadcasted_iota(jnp.int32, (tok_rows, tok_rows), 1)
        before = jnp.where(row <= col, 1.0, 0.0).astype(BF)
        place = jnp.dot(chosen.astype(BF), before, preferred_element_type=F32) * chosen
        high = weight.astype(BF).astype(F32)
        middle = (weight - high).astype(BF).astype(F32)
        low = weight - high - middle
        square[...] = jnp.zeros_like(square)
        square[:, :tok_rows] = jnp.where(
            kind == 0, place, jnp.where(kind == 1, high, jnp.where(kind == 2, middle, low))
        )
        tab_s[...] = square[...].T[:tok_rows].astype(BF)

    make_table()
    pl.semaphore_wait(barrier, len(near) + n_dp - 1)

    sends = []

    def launch(item):
        item.start()
        sends.append(item)

    def block(p, h=None):
        if h is None:
            return whole_ref.at[pl.ds(p * toks, toks), :]
        rows = toks // 2
        return whole_ref.at[pl.ds(p * toks + h * rows, rows), :]

    def own_slice(src, number):
        rows = pl.ds(pl.multiple_of(src * tok_rows, tok_rows), tok_rows)
        return whole_ref.at[rows, pl.ds(number * width, LANES if number == 2 else width)]

    def to_slice(m, number):
        q = (d + m) % n_dp
        cols = pl.ds(pl.multiple_of(q * width, LANES), width)
        source = tab_s if number == 2 else (tok_ref, grad_ref)[number].at[:, cols]
        target = own_slice(d, number)
        if m == 0:
            return pltpu.make_async_copy(source, target, local_sem.at[number])
        return pltpu.make_async_remote_copy(
            src_ref=source, dst_ref=target, send_sem=a2a_send.at[m - 1, number],
            recv_sem=a2a_recv.at[m - 1, number], device_id={"dp": q}, device_id_type=MESH,
        )

    def from_slice(m, number):
        ref = own_slice((d + n_dp - m) % n_dp, number)
        return pltpu.make_async_remote_copy(
            src_ref=ref, dst_ref=ref, send_sem=a2a_send.at[m - 1, number],
            recv_sem=a2a_recv.at[m - 1, number], device_id={"dp": (d + m) % n_dp}, device_id_type=MESH,
        )

    def spot(da, db, rel):
        return db * GROUP + da * 2 + rel

    def ag_copy_to(axis, way, da, db, h):
        step = SIDE - 1 if way == 0 else 1
        seen = 1 if way == 0 else SIDE - 1
        da2 = (da + seen) % SIDE if axis == 0 else da
        db2 = (db + seen) % SIDE if axis == 1 else db
        along_y = 1 - c if axis == 0 else c
        y2 = (y + step * along_y) % SIDE
        z2 = (z + step * (1 - along_y)) % SIDE
        return pltpu.make_async_remote_copy(
            src_ref=block(spot(da, db, 0), h),
            dst_ref=block(spot(da2, db2, 0), h),
            send_sem=ag_send.at[da * SIDE + db, axis * 2 + way, h],
            recv_sem=ag_recv.at[da2 * SIDE + db2, h],
            device_id={"expert": (y2 * SIDE + z2) * 2 + c},
            device_id_type=MESH,
        )

    def ag_wait(da, db, h):
        ref = block(spot(da, db, 0), h)
        pltpu.make_async_remote_copy(
            src_ref=ref, dst_ref=ref, send_sem=ag_send.at[0, 0, 0], recv_sem=ag_recv.at[da * SIDE + db, h],
            device_id={"expert": (e + 1) % experts}, device_id_type=MESH,
        ).wait_recv()

    def pair_copy(da, db):
        return pltpu.make_async_remote_copy(
            src_ref=block(spot(da, db, 0)), dst_ref=block(spot(da, db, 1)),
            send_sem=pair_send.at[da * SIDE + db], recv_sem=pair_recv.at[da * SIDE + db],
            device_id={"expert": e + 1 - 2 * c}, device_id_type=MESH,
        )

    def spread(axis, da, db):
        for way, h in ((0, 0), (1, 1), (0, 1), (1, 0)):
            launch(ag_copy_to(axis, way, da, db, h))

    def slices():
        for m in (1, 3, 2, 0):
            for number in range(3):
                to_slice(m, number).start()
        for number in range(3):
            to_slice(0, number).wait()
            for m in range(1, n_dp):
                from_slice(m, number).wait_recv()

    def mine_copy():
        return pltpu.make_async_copy(block(0), mine, local_sem.at[5])

    def own_phase():
        launch(pair_copy(0, 0))
        spread(0, 0, 0)
        mine_copy().start()

    def first_phase():
        ag_wait(1, 0, 0)
        launch(ag_copy_to(0, 0, 1, 0, 0))
        ag_wait(3, 0, 1)
        launch(ag_copy_to(0, 1, 3, 0, 1))
        spread(1, 0, 0)
        for da in (1, 3):
            ag_wait(da, 0, 1 if da == 1 else 0)
            launch(pair_copy(da, 0))
            spread(1, da, 0)
        ag_wait(2, 0, 0)
        ag_wait(2, 0, 1)
        launch(pair_copy(2, 0))
        spread(1, 2, 0)
        mine_copy().wait()

    def second_phase(da):
        ag_wait(da, 1, 0)
        launch(ag_copy_to(1, 0, da, 1, 0))
        ag_wait(da, 3, 1)
        launch(ag_copy_to(1, 1, da, 3, 1))
        ag_wait(da, 1, 1)
        launch(pair_copy(da, 1))
        ag_wait(da, 3, 0)
        launch(pair_copy(da, 3))

    def third_phase(da):
        ag_wait(da, 2, 0)
        ag_wait(da, 2, 1)
        launch(pair_copy(da, 2))

    def size_of(k):
        return CHUNKS[k][1] * slots_dp

    def rows_of(k, part_half=None):
        start = CHUNKS[k][0] * slots_dp
        if part_half is None:
            return pl.ds(start, size_of(k))
        return pl.ds(start + part_half * (size_of(k) // 2), size_of(k) // 2)

    def half_rows(k):
        return pl.ds(CHUNKS[k][0] * slots_dp // 2, size_of(k) // 2)

    def cols_of(q):
        return pl.ds(pl.multiple_of(q * quarter, quarter), quarter)

    def take_chunk(k):
        first, count = CHUNKS[k]
        for p in range(first, first + count):
            if p % 2 == 1:
                pair_copy((p // 2) % SIDE, p // GROUP).wait_recv()
        load = pltpu.make_async_copy(
            whole_ref.at[pl.ds(first * toks, count * toks), :], blk.at[pl.ds(0, count * toks), :], local_sem.at[3]
        )
        load.start()
        load.wait()
        pair_rows = 2 * slots_dp
        pair_toks = 2 * toks

        def one(i, carry):
            span = pl.ds(pl.multiple_of(i * pair_toks, pair_toks), pair_toks)
            line = lax.broadcasted_iota(jnp.int32, (16, LANES), 0)
            lane = lax.broadcasted_iota(jnp.int32, (16, LANES), 1)
            want = jnp.where((lane == line * experts + e) & (line < 4), 1.0, 0.0).astype(BF)
            found = dot32(want, blk[span, 2 * width :], ((1,), (1,)))
            place = found[0:1, :]
            scale = found[1:2, :] + found[2:3, :] + found[3:4, :]
            token = lax.broadcasted_iota(jnp.int32, (1, pair_toks), 1)
            base = (lax.shift_right_logical(token, tok_bits) * slots).astype(F32)
            goal = jnp.where(place > 0.0, base + place - 1.0, -1.0)
            row = lax.broadcasted_iota(jnp.int32, (pair_rows, pair_toks), 0).astype(F32)
            hit = row == goal
            picked = jnp.dot(
                jnp.where(hit, 1.0, 0.0).astype(BF), blk[span, : 2 * width], preferred_element_type=F32
            )
            scales = jnp.sum(jnp.where(hit, scale, 0.0), axis=1, keepdims=True)
            x_s[pl.ds(pl.multiple_of(i * pair_rows, pair_rows), pair_rows), :] = picked[:, :width].astype(BF)
            g_s[pl.ds(pl.multiple_of(first * slots_dp + i * pair_rows, pair_rows), pair_rows), :] = (
                picked[:, width:] * scales
            ).astype(BF)
            return carry

        lax.fori_loop(0, count // 2, one, 0)

    def copy(k, way, number, source, target):
        return pltpu.make_async_remote_copy(
            src_ref=source, dst_ref=target, send_sem=ring_send.at[k, way, number],
            recv_sem=ring_recv.at[k, way, number], device_id={"dp": to[way]}, device_id_type=MESH,
        )

    def toward(way):
        return part.at[2 if way == 0 else 0]

    def rs_copy(k, way, number):
        if number == 0:
            return copy(k, way, 0, part.at[1, :, rows_of(k, way), :], in_half.at[way, :, half_rows(k), :])
        h = way if number == 2 else 1 - way
        return copy(
            k, way, number, toward(way).at[:, rows_of(k, h), :], in_full.at[way, :, rows_of(k, h), :]
        )

    def ag_terms(k, way, number, q):
        h = way if number in (3, 5) else 1 - way
        ref = terms.at[:, rows_of(k, h), cols_of(q)]
        return copy(k, way, number, ref, ref)

    def ring_copy(k, way, number):
        return ag_terms(k, way, number, to[1 - way] if number == 5 else d)

    def ring_arrival(k, way, number):
        return ag_terms(k, way, number, (d + 2) % n_dp if number == 5 else to[1 - way])

    def partial(k, q, i):
        if i == 2:
            return dot32(g_s[rows_of(k), :], down_ref[cols_of(q), :], ((1,), (1,)))
        right = (gate_ref, up_ref)[i]
        return jnp.dot(x_s[pl.ds(0, size_of(k)), :], right[:, cols_of(q)], preferred_element_type=F32)

    def stage0(k):
        def one(step, carry):
            m = (step + 1) % (n_dp - 1)
            q = (d + m + 1) % n_dp
            for i in range(3):
                part[m, i, rows_of(k), :] = partial(k, q, i).astype(BF)
            return carry

        lax.fori_loop(0, n_dp - 1, one, 0)
        for number in range(2):
            for way in range(2):
                rs_copy(k, way, number).start()
        for i in range(3):
            own[i, rows_of(k), :] = partial(k, d, i)
        xt_s[:, rows_of(k)] = x_s[pl.ds(0, size_of(k)), :].T

    def stage1(k):
        for way in range(2):
            rs_copy(k, way, 0).wait_recv()
            m = 2 if way == 0 else 0
            for i in range(3):
                span = rows_of(k, way)
                total = part[m, i, span, :].astype(F32) + in_half[way, i, half_rows(k), :].astype(F32)
                part[m, i, span, :] = total.astype(BF)
            rs_copy(k, way, 2).start()

    def stage2(k):
        for number in (1, 2):
            for way in range(2):
                rs_copy(k, way, number).wait_recv()

        def total(i, span):
            return own[i, span, :] + in_full[0, i, span, :].astype(F32) + in_full[1, i, span, :].astype(F32)

        step_rows = 2 * slots_dp

        def act(step, carry):
            start = CHUNKS[k][0] * slots_dp + step * step_rows
            span = pl.ds(pl.multiple_of(start, step_rows), step_rows)
            gate = total(0, span)
            up = total(1, span)
            hgrad = total(2, span)
            sig = jax.nn.sigmoid(gate)
            val = gate * sig
            slope = sig * (1.0 + gate * (1.0 - sig))
            terms[0, span, cols_of(d)] = (val * up).astype(BF)
            terms[1, span, cols_of(d)] = (hgrad * up * slope).astype(BF)
            terms[2, span, cols_of(d)] = (hgrad * val).astype(BF)
            return carry

        lax.fori_loop(0, size_of(k) // step_rows, act, 0)
        for number in (3, 4):
            for way in range(2):
                ring_copy(k, way, number).start()

    def stage3(k):
        for way in range(2):
            ring_arrival(k, way, 3).wait_recv()
            ring_copy(k, way, 5).start()

    def home(p):
        return pl.ds(pl.multiple_of(p * slots_dp, slots_dp), slots_dp)

    def back_copy(k, i):
        db = CHUNKS[k][0] // GROUP
        p = CHUNKS[k][0] + i
        s = (c + p) % 2
        da = (p // 2) % SIDE
        y2 = (y + da * (1 - s) + db * s) % SIDE
        z2 = (z + db * (1 - s) + da * s) % SIDE
        return pltpu.make_async_remote_copy(
            src_ref=rows_out.at[home(p), :],
            dst_ref=back_ref.at[home(p), :],
            send_sem=ret_send.at[p],
            recv_sem=ret_recv.at[p],
            device_id={"expert": (y2 * SIDE + z2) * 2 + s},
            device_id_type=MESH,
        )

    def self_copy():
        return pltpu.make_async_copy(rows_out.at[home(0), :], back_ref.at[home(0), :], local_sem.at[4])

    def each_back(k, act):
        def one(i, carry):
            act(back_copy(k, i))
            return carry

        lax.fori_loop(1 if k == 0 else 0, CHUNKS[k][1], one, 0)

    def stage4(k):
        for number in (4, 5):
            for way in range(2):
                ring_arrival(k, way, number).wait_recv()
        half = size_of(k) // 2

        def one(h, carry):
            span = pl.ds(pl.multiple_of(CHUNKS[k][0] * slots_dp + h * half, slots_dp), half)
            rows_out[span, :width] = jnp.dot(
                terms[0, span, :], down_ref[...], preferred_element_type=F32
            ).astype(BF)
            rows_out[span, width:] = (
                dot32(terms[1, span, :], gate_ref[...], ((1,), (1,)))
                + dot32(terms[2, span, :], up_ref[...], ((1,), (1,)))
            ).astype(BF)
            return carry

        lax.fori_loop(0, 2, one, 0)
        if k == 0:
            self_copy().start()
        each_back(k, lambda item: item.start())
        hid_t[:, rows_of(k)] = terms[0, rows_of(k), :].T

    def fold(k):
        first, count = CHUNKS[k]
        rows = size_of(k)
        each_back(k, lambda item: item.wait_recv())
        if k == 0:
            self_copy().wait()
        load = pltpu.make_async_copy(back_ref.at[rows_of(k), :], bk.at[pl.ds(0, rows), :], local_sem.at[6])
        load.start()
        row = lax.broadcasted_iota(jnp.int32, (1, rows), 1)
        index = lax.shift_right_logical(row * (65536 // slots_dp + 1), 16)
        local = (row - index * slots_dp).astype(F32)
        p = first + index
        db = first // GROUP
        da = lax.shift_right_logical(p, 1) & (SIDE - 1)
        core = (c + p) & 1
        y2 = (y + 2 * SIDE - (da * (1 - c) + db * c)) & (SIDE - 1)
        z2 = (z + 2 * SIDE - (db * (1 - c) + da * c)) & (SIDE - 1)
        sender = (y2 * SIDE + z2) * 2 + core
        lane = lax.broadcasted_iota(jnp.int32, (LANES, rows), 0)
        names = [jnp.where(lane == kind * experts + sender, 1.0, 0.0) for kind in range(4)]
        table = mine[:, 2 * width :]
        found = [jnp.dot(table, name.astype(BF), preferred_element_type=F32) for name in names]
        token = lax.broadcasted_iota(jnp.int32, (toks, rows), 0)
        base = (lax.shift_right_logical(token, tok_bits) * slots).astype(F32)
        hit = (found[0] > 0.0) & (local == base + found[0] - 1.0)
        scaled = jnp.concatenate([jnp.where(hit, found[i], 0.0).astype(BF) for i in (1, 2, 3)], axis=0)
        once = jnp.where(hit, 1.0, 0.0).astype(BF)
        load.wait()
        outs = bk[pl.ds(0, rows), :width]
        three = jnp.dot(scaled, outs, preferred_element_type=F32)
        mixed = three[:toks] + three[toks : 2 * toks] + three[2 * toks :]
        tgrad = jnp.dot(once, bk[pl.ds(0, rows), width:], preferred_element_type=F32)
        dots = dot32(mine[:, width : 2 * width], outs, ((1,), (1,)))
        route = dot32(jnp.where(hit, dots, 0.0), names[0], ((1,), (1,)), lax.Precision.HIGHEST)
        if k == 0:
            mixed_acc[...] = mixed
            tgrad_acc[...] = tgrad
            route_acc[...] = route
        else:
            mixed_acc[...] += mixed
            tgrad_acc[...] += tgrad
            route_acc[...] += route

    def weight_grads():
        span = stage_a.shape[2]
        tall = stage_b.shape[1]

        def out_copy(kind, i, slot):
            if kind == 2:
                target = down_out.at[pl.ds(pl.multiple_of(i * tall, tall), tall), :]
                return pltpu.make_async_copy(stage_b.at[slot], target, stage_sem.at[kind, slot])
            target = (gate_out, up_out)[kind].at[:, pl.ds(pl.multiple_of(i * span, span), span)]
            return pltpu.make_async_copy(stage_a.at[slot], target, stage_sem.at[kind, slot])

        for kind in range(3):
            count = gate_ref.shape[1] // (tall if kind == 2 else span)

            def one(i, carry, kind=kind):
                slot = i % 2

                @pl.when(i >= 2)
                def _():
                    out_copy(kind, i - 2, slot).wait()

                if kind == 2:
                    left = hid_t[pl.ds(pl.multiple_of(i * tall, tall), tall), :]
                    stage_b[slot] = jnp.dot(left, g_s[...], preferred_element_type=F32).astype(BF)
                else:
                    right = terms[1 + kind, :, pl.ds(pl.multiple_of(i * span, span), span)]
                    stage_a[slot] = jnp.dot(xt_s[...], right, preferred_element_type=F32).astype(BF)
                out_copy(kind, i, slot).start()
                return carry

            lax.fori_loop(0, count, one, 0)
            out_copy(kind, count - 2, count % 2).wait()
            out_copy(kind, count - 1, (count - 1) % 2).wait()

    def final_copy(m, number):
        q = (d + m) % n_dp
        rows = pl.ds(pl.multiple_of(q * tok_rows, tok_rows), tok_rows)
        if number == 2:
            source, target = route_acc.at[rows, :], route_in.at[d]
        else:
            source = final_v.at[rows, pl.ds(number * width, width)]
            target = (mixed_out, tgrad_out)[number].at[:, pl.ds(pl.multiple_of(d * width, LANES), width)]
        if m == 0:
            return pltpu.make_async_copy(source, target, fin_send.at[m, number])
        return pltpu.make_async_remote_copy(
            src_ref=source, dst_ref=target, send_sem=fin_send.at[m, number],
            recv_sem=fin_recv.at[m - 1, number], device_id={"dp": q}, device_id_type=MESH,
        )

    def final_arrival(m, number):
        src = (d + n_dp - m) % n_dp
        if number == 2:
            ref = route_in.at[src]
        else:
            ref = (mixed_out, tgrad_out)[number].at[:, pl.ds(pl.multiple_of(src * width, LANES), width)]
        return pltpu.make_async_remote_copy(
            src_ref=ref, dst_ref=ref, send_sem=fin_send.at[m, number],
            recv_sem=fin_recv.at[m - 1, number], device_id={"dp": (d + m) % n_dp}, device_id_type=MESH,
        )

    def finish():
        final_v[:, :width] = mixed_acc[...].astype(BF)
        final_v[:, width:] = tgrad_acc[...].astype(BF)
        for m in (2, 1, 3, 0):
            for number in range(3):
                final_copy(m, number).start()
        for number in (2, 0, 1):
            final_copy(0, number).wait()
            for m in range(1, n_dp):
                final_arrival(m, number).wait_recv()
        total = route_in[0]
        for q in range(1, n_dp):
            total = total + route_in[q]
        square[:tok_rows, :] = total
        turned = square[...].T[:, :tok_rows]
        line = lax.broadcasted_iota(jnp.int32, (LANES, tok_rows), 0)
        place = lax.broadcasted_iota(jnp.int32, (top, tok_rows), 0)
        result = jnp.zeros((top, tok_rows), F32)
        for k in range(top):
            row = jnp.sum(jnp.where(line == ids_ref[k : k + 1, :], turned, 0.0), axis=0, keepdims=True)
            result = jnp.where(place == k, row, result)
        route_out[...] = result

    slices()
    own_phase()
    last = len(CHUNKS)
    for item in loads:
        item.wait()
    take_chunk(0)
    stage0(0)
    first_phase()
    for k in range(last + 1):
        if k < last:
            stage1(k)
        if k >= 1:
            stage3(k - 1)
        if k + 1 < last:
            take_chunk(k + 1)
            stage0(k + 1)
        if k == 0:
            second_phase(0)
            second_phase(1)
            stage2(0)
            second_phase(3)
            second_phase(2)
        if 1 <= k < last:
            stage2(k)
        if k == 1:
            for da in (0, 1, 3, 2):
                third_phase(da)
        if k == last:
            fold(last - 4)
        if k >= 1:
            stage4(k - 1)
        if 2 <= k <= last - 3:
            fold(k - 2)
    weight_grads()
    fold(last - 3)
    fold(last - 2)
    fold(last - 1)
    finish()

    for m in range(1, n_dp):
        for number in range(3):
            to_slice(m, number).wait_send()
            final_copy(m, number).wait_send()
    for item in sends:
        item.wait_send()
    for k in range(last):
        for way in range(2):
            for number in range(3):
                rs_copy(k, way, number).wait_send()
                ring_copy(k, way, number + 3).wait_send()
        each_back(k, lambda item: item.wait_send())


def moe(tokens, out_grad, ids, weights, gate, up, down, experts, n_dp):
    width, hidden = gate.shape
    tok_rows, top = ids.shape
    slots = min(tok_rows, 3 * tok_rows * top // (2 * experts))
    toks = n_dp * tok_rows
    slots_dp = n_dp * slots
    rows = experts * slots_dp
    quarter = hidden // n_dp
    chunk = GROUP * slots_dp
    both = 2 * width
    last = len(CHUNKS)
    dma = pltpu.SemaphoreType.DMA
    vmem = pltpu.VMEM
    anywhere = pl.BlockSpec(memory_space=pl.ANY)
    inside = pl.BlockSpec(memory_space=pltpu.VMEM)
    return pl.pallas_call(
        moe_kernel,
        out_shape=(
            jax.ShapeDtypeStruct(tokens.shape, BF),
            jax.ShapeDtypeStruct(tokens.shape, BF),
            jax.ShapeDtypeStruct((top, tok_rows), F32),
            jax.ShapeDtypeStruct((width, hidden), BF),
            jax.ShapeDtypeStruct((width, hidden), BF),
            jax.ShapeDtypeStruct((hidden, width), BF),
            jax.ShapeDtypeStruct((rows, both), BF),
            jax.ShapeDtypeStruct((experts * toks, both + LANES), BF),
        ),
        in_specs=[anywhere, anywhere, inside, inside, anywhere, anywhere, anywhere],
        out_specs=(anywhere, anywhere, inside) + (anywhere,) * 5,
        scratch_shapes=[
            vmem((width, hidden), BF),
            vmem((width, hidden), BF),
            vmem((hidden, width), BF),
            vmem((LANES, LANES), F32),
            vmem((tok_rows, LANES), BF),
            vmem((toks, both + LANES), BF),
            vmem((GROUP * toks, both + LANES), BF),
            vmem((chunk, width), BF),
            vmem((width, rows), BF),
            vmem((rows, width), BF),
            vmem((hidden, rows), BF),
            vmem((n_dp - 1, 3, rows, quarter), BF),
            vmem((3, rows, quarter), F32),
            vmem((2, 3, rows // 2, quarter), BF),
            vmem((2, 3, rows, quarter), BF),
            vmem((3, rows, hidden), BF),
            vmem((rows, both), BF),
            vmem((2, width, quarter), BF),
            vmem((2, quarter, width), BF),
            vmem((chunk, both), BF),
            vmem((toks, width), F32),
            vmem((toks, width), F32),
            vmem((toks, LANES), F32),
            vmem((toks, both), BF),
            vmem((n_dp, tok_rows, LANES), F32),
            dma((last, 2, 6)),
            dma((last, 2, 6)),
            dma((experts,)),
            dma((experts,)),
            dma((n_dp - 1, 3)),
            dma((n_dp - 1, 3)),
            dma((SIDE * SIDE, 4, 2)),
            dma((SIDE * SIDE, 2)),
            dma((SIDE * SIDE,)),
            dma((SIDE * SIDE,)),
            dma((10,)),
            dma((3, 2)),
            dma((n_dp, 3)),
            dma((n_dp - 1, 3)),
        ],
        compiler_params=pltpu.CompilerParams(
            collective_id=0, has_side_effects=True, vmem_limit_bytes=67043328
        ),
    )(tokens, out_grad, ids.T, weights.T, gate, up, down)


def per_device(tokens, ids, weights, out_grad, gate_weight, up_weight, down_weight):
    experts = lax.axis_size("expert")
    n_dp = lax.axis_size("dp")
    mixed, tgrad, route, gate_grad, up_grad, down_grad, _, _ = moe(
        tokens, out_grad, ids, weights, gate_weight[0], up_weight[0], down_weight[0], experts, n_dp
    )
    return (mixed, tgrad, route.T, gate_grad[None], up_grad[None], down_grad[None])


def solution(mesh):
    rows = P(("dp", "expert"), None)
    weights = (P("expert", "dp", None), P("expert", "dp", None), P("expert", None, "dp"))
    return jax.shard_map(
        per_device,
        mesh=mesh,
        in_specs=(rows, rows, rows, rows) + weights,
        out_specs=(rows, rows, rows) + weights,
        check_vma=False,
    )
```

```python
import jax
import jax.numpy as jnp
from jax import lax
from jax.experimental import pallas as pl
from jax.experimental.pallas import tpu as pltpu
from jax.sharding import PartitionSpec as P

BF = jnp.bfloat16
F32 = jnp.float32
LANES = 128
SIDE = 4
GROUP = 8
CHUNKS = ((0, 2), (2, 4), (8, 8), (16, 8), (24, 4), (28, 4), (6, 2))
MESH = pl.DeviceIdType.MESH


def dot32(a, b, dims, precision=None):
    return lax.dot_general(a, b, (dims, ((), ())), precision=precision, preferred_element_type=F32)


def moe_kernel(
    tok_ref, grad_ref, ids_ref, wts_ref, gate_hbm, up_hbm, down_hbm,
    mixed_out, tgrad_out, route_out, gate_out, up_out, down_out, back_ref, whole_ref,
    gate_ref, up_ref, down_ref, square, tab_s, mine, blk, x_s, xt_s, g_s, hid_t, part, own, in_half, in_full, terms, rows_out, stage_a, stage_b,
    bk, mixed_acc, tgrad_acc, route_acc, final_v, route_in,
    ring_send, ring_recv, ret_send, ret_recv, a2a_send, a2a_recv, ag_send, ag_recv,
    pair_send, pair_recv, local_sem, stage_sem, fin_send, fin_recv,
):
    n_dp = lax.axis_size("dp")
    experts = lax.axis_size("expert")
    d = lax.axis_index("dp")
    e = lax.axis_index("expert")
    y = e // (2 * SIDE)
    z = (e // 2) % SIDE
    c = e % 2
    top, tok_rows = ids_ref.shape
    toks = n_dp * tok_rows
    tok_bits = tok_rows.bit_length() - 1
    slots_dp = rows_out.shape[0] // experts
    slots = slots_dp // n_dp
    quarter = own.shape[2]
    width = gate_ref.shape[0]
    to = ((d + n_dp - 1) % n_dp, (d + 1) % n_dp)

    barrier = pltpu.get_barrier_semaphore()
    for m in range(1, n_dp):
        pl.semaphore_signal(barrier, inc=1, device_id={"dp": (d + m) % n_dp}, device_id_type=MESH)

    loads = [
        pltpu.make_async_copy(source, target, local_sem.at[7 + i])
        for i, (source, target) in enumerate(((gate_hbm, gate_ref), (up_hbm, up_ref), (down_hbm, down_ref)))
    ]
    for item in loads:
        item.start()

    near = [e + 1 - 2 * c]
    for step in (1, SIDE - 1):
        near.append((((y + step) % SIDE) * SIDE + z) * 2 + c)
        near.append((y * SIDE + (z + step) % SIDE) * 2 + c)
    for peer in near:
        pl.semaphore_signal(barrier, inc=1, device_id={"expert": peer}, device_id_type=MESH)

    def make_table():
        line = lax.broadcasted_iota(jnp.int32, (LANES, tok_rows), 0)
        name = line & (experts - 1)
        kind = lax.shift_right_logical(line, experts.bit_length() - 1)
        chosen = jnp.zeros((LANES, tok_rows), F32)
        weight = jnp.zeros((LANES, tok_rows), F32)
        for k in range(top):
            same = ids_ref[k : k + 1, :] == name
            chosen += jnp.where(same, 1.0, 0.0)
            weight += jnp.where(same, wts_ref[k : k + 1, :], 0.0)
        row = lax.broadcasted_iota(jnp.int32, (tok_rows, tok_rows), 0)
        col = lax.broadcasted_iota(jnp.int32, (tok_rows, tok_rows), 1)
        before = jnp.where(row <= col, 1.0, 0.0).astype(BF)
        place = jnp.dot(chosen.astype(BF), before, preferred_element_type=F32) * chosen
        high = weight.astype(BF).astype(F32)
        middle = (weight - high).astype(BF).astype(F32)
        low = weight - high - middle
        square[...] = jnp.zeros_like(square)
        square[:, :tok_rows] = jnp.where(
            kind == 0, place, jnp.where(kind == 1, high, jnp.where(kind == 2, middle, low))
        )
        tab_s[...] = square[...].T[:tok_rows].astype(BF)

    make_table()
    pl.semaphore_wait(barrier, len(near) + n_dp - 1)

    sends = []

    def launch(item):
        item.start()
        sends.append(item)

    def block(p, h=None):
        if h is None:
            return whole_ref.at[pl.ds(p * toks, toks), :]
        rows = toks // 2
        return whole_ref.at[pl.ds(p * toks + h * rows, rows), :]

    def own_slice(src, number):
        rows = pl.ds(pl.multiple_of(src * tok_rows, tok_rows), tok_rows)
        return whole_ref.at[rows, pl.ds(number * width, LANES if number == 2 else width)]

    def to_slice(m, number):
        q = (d + m) % n_dp
        cols = pl.ds(pl.multiple_of(q * width, LANES), width)
        source = tab_s if number == 2 else (tok_ref, grad_ref)[number].at[:, cols]
        target = own_slice(d, number)
        if m == 0:
            return pltpu.make_async_copy(source, target, local_sem.at[number])
        return pltpu.make_async_remote_copy(
            src_ref=source, dst_ref=target, send_sem=a2a_send.at[m - 1, number],
            recv_sem=a2a_recv.at[m - 1, number], device_id={"dp": q}, device_id_type=MESH,
        )

    def from_slice(m, number):
        ref = own_slice((d + n_dp - m) % n_dp, number)
        return pltpu.make_async_remote_copy(
            src_ref=ref, dst_ref=ref, send_sem=a2a_send.at[m - 1, number],
            recv_sem=a2a_recv.at[m - 1, number], device_id={"dp": (d + m) % n_dp}, device_id_type=MESH,
        )

    def spot(da, db, rel):
        return db * GROUP + da * 2 + rel

    def ag_copy_to(axis, way, da, db, h):
        step = SIDE - 1 if way == 0 else 1
        seen = 1 if way == 0 else SIDE - 1
        da2 = (da + seen) % SIDE if axis == 0 else da
        db2 = (db + seen) % SIDE if axis == 1 else db
        along_y = 1 - c if axis == 0 else c
        y2 = (y + step * along_y) % SIDE
        z2 = (z + step * (1 - along_y)) % SIDE
        return pltpu.make_async_remote_copy(
            src_ref=block(spot(da, db, 0), h),
            dst_ref=block(spot(da2, db2, 0), h),
            send_sem=ag_send.at[da * SIDE + db, axis * 2 + way, h],
            recv_sem=ag_recv.at[da2 * SIDE + db2, h],
            device_id={"expert": (y2 * SIDE + z2) * 2 + c},
            device_id_type=MESH,
        )

    def ag_wait(da, db, h):
        ref = block(spot(da, db, 0), h)
        pltpu.make_async_remote_copy(
            src_ref=ref, dst_ref=ref, send_sem=ag_send.at[0, 0, 0], recv_sem=ag_recv.at[da * SIDE + db, h],
            device_id={"expert": (e + 1) % experts}, device_id_type=MESH,
        ).wait_recv()

    def pair_copy(da, db):
        return pltpu.make_async_remote_copy(
            src_ref=block(spot(da, db, 0)), dst_ref=block(spot(da, db, 1)),
            send_sem=pair_send.at[da * SIDE + db], recv_sem=pair_recv.at[da * SIDE + db],
            device_id={"expert": e + 1 - 2 * c}, device_id_type=MESH,
        )

    def spread(axis, da, db):
        for way, h in ((0, 0), (1, 1), (0, 1), (1, 0)):
            launch(ag_copy_to(axis, way, da, db, h))

    def slices():
        for m in (1, 3, 2, 0):
            for number in range(3):
                to_slice(m, number).start()
        for number in range(3):
            to_slice(0, number).wait()
            for m in range(1, n_dp):
                from_slice(m, number).wait_recv()

    def mine_copy():
        return pltpu.make_async_copy(block(0), mine, local_sem.at[5])

    def own_phase():
        launch(pair_copy(0, 0))
        spread(0, 0, 0)
        mine_copy().start()

    def first_phase():
        ag_wait(1, 0, 0)
        launch(ag_copy_to(0, 0, 1, 0, 0))
        ag_wait(3, 0, 1)
        launch(ag_copy_to(0, 1, 3, 0, 1))
        spread(1, 0, 0)
        for da in (1, 3):
            ag_wait(da, 0, 1 if da == 1 else 0)
            launch(pair_copy(da, 0))
            spread(1, da, 0)
        ag_wait(2, 0, 0)
        ag_wait(2, 0, 1)
        launch(pair_copy(2, 0))
        spread(1, 2, 0)
        mine_copy().wait()

    def second_phase(da):
        ag_wait(da, 1, 0)
        launch(ag_copy_to(1, 0, da, 1, 0))
        ag_wait(da, 3, 1)
        launch(ag_copy_to(1, 1, da, 3, 1))
        ag_wait(da, 1, 1)
        launch(pair_copy(da, 1))
        ag_wait(da, 3, 0)
        launch(pair_copy(da, 3))

    def third_phase(da):
        ag_wait(da, 2, 0)
        ag_wait(da, 2, 1)
        launch(pair_copy(da, 2))

    def size_of(k):
        return CHUNKS[k][1] * slots_dp

    def rows_of(k, part_half=None):
        start = CHUNKS[k][0] * slots_dp
        if part_half is None:
            return pl.ds(start, size_of(k))
        return pl.ds(start + part_half * (size_of(k) // 2), size_of(k) // 2)

    def half_rows(k):
        return pl.ds(CHUNKS[k][0] * slots_dp // 2, size_of(k) // 2)

    def cols_of(q):
        return pl.ds(pl.multiple_of(q * quarter, quarter), quarter)

    def take_chunk(k):
        first, count = CHUNKS[k]
        for p in range(first, first + count):
            if p % 2 == 1:
                pair_copy((p // 2) % SIDE, p // GROUP).wait_recv()
        load = pltpu.make_async_copy(
            whole_ref.at[pl.ds(first * toks, count * toks), :], blk.at[pl.ds(0, count * toks), :], local_sem.at[3]
        )
        load.start()
        load.wait()
        pair_rows = 2 * slots_dp
        pair_toks = 2 * toks

        def one(i, carry):
            span = pl.ds(pl.multiple_of(i * pair_toks, pair_toks), pair_toks)
            line = lax.broadcasted_iota(jnp.int32, (16, LANES), 0)
            lane = lax.broadcasted_iota(jnp.int32, (16, LANES), 1)
            want = jnp.where((lane == line * experts + e) & (line < 4), 1.0, 0.0).astype(BF)
            found = dot32(want, blk[span, 2 * width :], ((1,), (1,)))
            place = found[0:1, :]
            scale = found[1:2, :] + found[2:3, :] + found[3:4, :]
            token = lax.broadcasted_iota(jnp.int32, (1, pair_toks), 1)
            base = (lax.shift_right_logical(token, tok_bits) * slots).astype(F32)
            goal = jnp.where(place > 0.0, base + place - 1.0, -1.0)
            row = lax.broadcasted_iota(jnp.int32, (pair_rows, pair_toks), 0).astype(F32)
            hit = row == goal
            picked = jnp.dot(
                jnp.where(hit, 1.0, 0.0).astype(BF), blk[span, : 2 * width], preferred_element_type=F32
            )
            scales = jnp.sum(jnp.where(hit, scale, 0.0), axis=1, keepdims=True)
            x_s[pl.ds(pl.multiple_of(i * pair_rows, pair_rows), pair_rows), :] = picked[:, :width].astype(BF)
            g_s[pl.ds(pl.multiple_of(first * slots_dp + i * pair_rows, pair_rows), pair_rows), :] = (
                picked[:, width:] * scales
            ).astype(BF)
            return carry

        lax.fori_loop(0, count // 2, one, 0)

    def copy(k, way, number, source, target):
        return pltpu.make_async_remote_copy(
            src_ref=source, dst_ref=target, send_sem=ring_send.at[k, way, number],
            recv_sem=ring_recv.at[k, way, number], device_id={"dp": to[way]}, device_id_type=MESH,
        )

    def toward(way):
        return part.at[2 if way == 0 else 0]

    def rs_copy(k, way, number):
        if number == 0:
            return copy(k, way, 0, part.at[1, :, rows_of(k, way), :], in_half.at[way, :, half_rows(k), :])
        h = way if number == 2 else 1 - way
        return copy(
            k, way, number, toward(way).at[:, rows_of(k, h), :], in_full.at[way, :, rows_of(k, h), :]
        )

    def ag_terms(k, way, number, q):
        h = way if number in (3, 5) else 1 - way
        ref = terms.at[:, rows_of(k, h), cols_of(q)]
        return copy(k, way, number, ref, ref)

    def ring_copy(k, way, number):
        return ag_terms(k, way, number, to[1 - way] if number == 5 else d)

    def ring_arrival(k, way, number):
        return ag_terms(k, way, number, (d + 2) % n_dp if number == 5 else to[1 - way])

    def partial(k, q, i):
        if i == 2:
            return dot32(g_s[rows_of(k), :], down_ref[cols_of(q), :], ((1,), (1,)))
        right = (gate_ref, up_ref)[i]
        return jnp.dot(x_s[pl.ds(0, size_of(k)), :], right[:, cols_of(q)], preferred_element_type=F32)

    def stage0(k):
        def one(step, carry):
            m = (step + 1) % (n_dp - 1)
            q = (d + m + 1) % n_dp
            for i in range(3):
                part[m, i, rows_of(k), :] = partial(k, q, i).astype(BF)
            return carry

        lax.fori_loop(0, n_dp - 1, one, 0)
        for number in range(2):
            for way in range(2):
                rs_copy(k, way, number).start()
        for i in range(3):
            own[i, rows_of(k), :] = partial(k, d, i)
        xt_s[:, rows_of(k)] = x_s[pl.ds(0, size_of(k)), :].T

    def stage1(k):
        for way in range(2):
            rs_copy(k, way, 0).wait_recv()
            m = 2 if way == 0 else 0
            for i in range(3):
                span = rows_of(k, way)
                total = part[m, i, span, :].astype(F32) + in_half[way, i, half_rows(k), :].astype(F32)
                part[m, i, span, :] = total.astype(BF)
            rs_copy(k, way, 2).start()

    def stage2(k):
        for number in (1, 2):
            for way in range(2):
                rs_copy(k, way, number).wait_recv()

        def total(i, span):
            return own[i, span, :] + in_full[0, i, span, :].astype(F32) + in_full[1, i, span, :].astype(F32)

        step_rows = 2 * slots_dp

        def act(step, carry):
            start = CHUNKS[k][0] * slots_dp + step * step_rows
            span = pl.ds(pl.multiple_of(start, step_rows), step_rows)
            gate = total(0, span)
            up = total(1, span)
            hgrad = total(2, span)
            sig = jax.nn.sigmoid(gate)
            val = gate * sig
            slope = sig * (1.0 + gate * (1.0 - sig))
            terms[0, span, cols_of(d)] = (val * up).astype(BF)
            terms[1, span, cols_of(d)] = (hgrad * up * slope).astype(BF)
            terms[2, span, cols_of(d)] = (hgrad * val).astype(BF)
            return carry

        lax.fori_loop(0, size_of(k) // step_rows, act, 0)
        for number in (3, 4):
            for way in range(2):
                ring_copy(k, way, number).start()

    def stage3(k):
        for way in range(2):
            ring_arrival(k, way, 3).wait_recv()
            ring_copy(k, way, 5).start()

    def home(p):
        return pl.ds(pl.multiple_of(p * slots_dp, slots_dp), slots_dp)

    def back_copy(k, i):
        db = CHUNKS[k][0] // GROUP
        p = CHUNKS[k][0] + i
        s = (c + p) % 2
        da = (p // 2) % SIDE
        y2 = (y + da * (1 - s) + db * s) % SIDE
        z2 = (z + db * (1 - s) + da * s) % SIDE
        return pltpu.make_async_remote_copy(
            src_ref=rows_out.at[home(p), :],
            dst_ref=back_ref.at[home(p), :],
            send_sem=ret_send.at[p],
            recv_sem=ret_recv.at[p],
            device_id={"expert": (y2 * SIDE + z2) * 2 + s},
            device_id_type=MESH,
        )

    def self_copy():
        return pltpu.make_async_copy(rows_out.at[home(0), :], back_ref.at[home(0), :], local_sem.at[4])

    def each_back(k, act):
        def one(i, carry):
            act(back_copy(k, i))
            return carry

        lax.fori_loop(1 if k == 0 else 0, CHUNKS[k][1], one, 0)

    def stage4(k):
        for number in (4, 5):
            for way in range(2):
                ring_arrival(k, way, number).wait_recv()
        half = size_of(k) // 2

        def one(h, carry):
            span = pl.ds(pl.multiple_of(CHUNKS[k][0] * slots_dp + h * half, slots_dp), half)
            rows_out[span, :width] = jnp.dot(
                terms[0, span, :], down_ref[...], preferred_element_type=F32
            ).astype(BF)
            rows_out[span, width:] = (
                dot32(terms[1, span, :], gate_ref[...], ((1,), (1,)))
                + dot32(terms[2, span, :], up_ref[...], ((1,), (1,)))
            ).astype(BF)
            return carry

        lax.fori_loop(0, 2, one, 0)
        if k == 0:
            self_copy().start()
        each_back(k, lambda item: item.start())
        hid_t[:, rows_of(k)] = terms[0, rows_of(k), :].T

    def fold(k):
        first, count = CHUNKS[k]
        rows = size_of(k)
        each_back(k, lambda item: item.wait_recv())
        if k == 0:
            self_copy().wait()
        load = pltpu.make_async_copy(back_ref.at[rows_of(k), :], bk.at[pl.ds(0, rows), :], local_sem.at[6])
        load.start()
        row = lax.broadcasted_iota(jnp.int32, (1, rows), 1)
        index = lax.shift_right_logical(row * (65536 // slots_dp + 1), 16)
        local = (row - index * slots_dp).astype(F32)
        p = first + index
        db = first // GROUP
        da = lax.shift_right_logical(p, 1) & (SIDE - 1)
        core = (c + p) & 1
        y2 = (y + 2 * SIDE - (da * (1 - c) + db * c)) & (SIDE - 1)
        z2 = (z + 2 * SIDE - (db * (1 - c) + da * c)) & (SIDE - 1)
        sender = (y2 * SIDE + z2) * 2 + core
        lane = lax.broadcasted_iota(jnp.int32, (LANES, rows), 0)
        names = [jnp.where(lane == kind * experts + sender, 1.0, 0.0) for kind in range(4)]
        table = mine[:, 2 * width :]
        found = [jnp.dot(table, name.astype(BF), preferred_element_type=F32) for name in names]
        token = lax.broadcasted_iota(jnp.int32, (toks, rows), 0)
        base = (lax.shift_right_logical(token, tok_bits) * slots).astype(F32)
        hit = (found[0] > 0.0) & (local == base + found[0] - 1.0)
        scaled = jnp.concatenate([jnp.where(hit, found[i], 0.0).astype(BF) for i in (1, 2, 3)], axis=0)
        once = jnp.where(hit, 1.0, 0.0).astype(BF)
        load.wait()
        outs = bk[pl.ds(0, rows), :width]
        three = jnp.dot(scaled, outs, preferred_element_type=F32)
        mixed = three[:toks] + three[toks : 2 * toks] + three[2 * toks :]
        tgrad = jnp.dot(once, bk[pl.ds(0, rows), width:], preferred_element_type=F32)
        dots = dot32(mine[:, width : 2 * width], outs, ((1,), (1,)))
        route = dot32(jnp.where(hit, dots, 0.0), names[0], ((1,), (1,)), lax.Precision.HIGHEST)
        if k == 0:
            mixed_acc[...] = mixed
            tgrad_acc[...] = tgrad
            route_acc[...] = route
        else:
            mixed_acc[...] += mixed
            tgrad_acc[...] += tgrad
            route_acc[...] += route

    def weight_grads():
        span = stage_a.shape[2]
        tall = stage_b.shape[1]

        def out_copy(kind, i, slot):
            if kind == 2:
                target = down_out.at[pl.ds(pl.multiple_of(i * tall, tall), tall), :]
                return pltpu.make_async_copy(stage_b.at[slot], target, stage_sem.at[kind, slot])
            target = (gate_out, up_out)[kind].at[:, pl.ds(pl.multiple_of(i * span, span), span)]
            return pltpu.make_async_copy(stage_a.at[slot], target, stage_sem.at[kind, slot])

        for kind in range(3):
            count = gate_ref.shape[1] // (tall if kind == 2 else span)

            def one(i, carry, kind=kind):
                slot = i % 2

                @pl.when(i >= 2)
                def _():
                    out_copy(kind, i - 2, slot).wait()

                if kind == 2:
                    left = hid_t[pl.ds(pl.multiple_of(i * tall, tall), tall), :]
                    stage_b[slot] = jnp.dot(left, g_s[...], preferred_element_type=F32).astype(BF)
                else:
                    right = terms[1 + kind, :, pl.ds(pl.multiple_of(i * span, span), span)]
                    stage_a[slot] = jnp.dot(xt_s[...], right, preferred_element_type=F32).astype(BF)
                out_copy(kind, i, slot).start()
                return carry

            lax.fori_loop(0, count, one, 0)
            out_copy(kind, count - 2, count % 2).wait()
            out_copy(kind, count - 1, (count - 1) % 2).wait()

    def final_copy(m, number):
        q = (d + m) % n_dp
        rows = pl.ds(pl.multiple_of(q * tok_rows, tok_rows), tok_rows)
        if number == 2:
            source, target = route_acc.at[rows, :], route_in.at[d]
        else:
            source = final_v.at[rows, pl.ds(number * width, width)]
            target = (mixed_out, tgrad_out)[number].at[:, pl.ds(pl.multiple_of(d * width, LANES), width)]
        if m == 0:
            return pltpu.make_async_copy(source, target, fin_send.at[m, number])
        return pltpu.make_async_remote_copy(
            src_ref=source, dst_ref=target, send_sem=fin_send.at[m, number],
            recv_sem=fin_recv.at[m - 1, number], device_id={"dp": q}, device_id_type=MESH,
        )

    def final_arrival(m, number):
        src = (d + n_dp - m) % n_dp
        if number == 2:
            ref = route_in.at[src]
        else:
            ref = (mixed_out, tgrad_out)[number].at[:, pl.ds(pl.multiple_of(src * width, LANES), width)]
        return pltpu.make_async_remote_copy(
            src_ref=ref, dst_ref=ref, send_sem=fin_send.at[m, number],
            recv_sem=fin_recv.at[m - 1, number], device_id={"dp": (d + m) % n_dp}, device_id_type=MESH,
        )

    def finish():
        final_v[:, :width] = mixed_acc[...].astype(BF)
        final_v[:, width:] = tgrad_acc[...].astype(BF)
        for m in (2, 1, 3, 0):
            for number in range(3):
                final_copy(m, number).start()
        for number in (2, 0, 1):
            final_copy(0, number).wait()
            for m in range(1, n_dp):
                final_arrival(m, number).wait_recv()
        total = route_in[0]
        for q in range(1, n_dp):
            total = total + route_in[q]
        square[:tok_rows, :] = total
        turned = square[...].T[:, :tok_rows]
        line = lax.broadcasted_iota(jnp.int32, (LANES, tok_rows), 0)
        place = lax.broadcasted_iota(jnp.int32, (top, tok_rows), 0)
        result = jnp.zeros((top, tok_rows), F32)
        for k in range(top):
            row = jnp.sum(jnp.where(line == ids_ref[k : k + 1, :], turned, 0.0), axis=0, keepdims=True)
            result = jnp.where(place == k, row, result)
        route_out[...] = result

    slices()
    own_phase()
    last = len(CHUNKS)
    for item in loads:
        item.wait()
    take_chunk(0)
    stage0(0)
    first_phase()
    for k in range(last + 1):
        if k < last and k != 1:
            stage1(k)
        if k > 1:
            stage3(k - 1)
        if k == 1:
            stage2(1)
        if k + 1 < last:
            take_chunk(k + 1)
            stage0(k + 1)
        if k == 0:
            second_phase(0)
            second_phase(1)
            stage2(0)
            stage1(1)
            second_phase(3)
            stage3(0)
            second_phase(2)
        if 2 <= k < last:
            stage2(k)
        if k == 1:
            for da in (0, 1, 3, 2):
                third_phase(da)
        if k == last:
            fold(last - 4)
        if k >= 1:
            stage4(k - 1)
        if 2 <= k <= last - 3:
            fold(k - 2)
    weight_grads()
    fold(last - 3)
    fold(last - 2)
    fold(last - 1)
    finish()

    for m in range(1, n_dp):
        for number in range(3):
            to_slice(m, number).wait_send()
            final_copy(m, number).wait_send()
    for item in sends:
        item.wait_send()
    for k in range(last):
        for way in range(2):
            for number in range(3):
                rs_copy(k, way, number).wait_send()
                ring_copy(k, way, number + 3).wait_send()
        each_back(k, lambda item: item.wait_send())


def moe(tokens, out_grad, ids, weights, gate, up, down, experts, n_dp):
    width, hidden = gate.shape
    tok_rows, top = ids.shape
    slots = min(tok_rows, 3 * tok_rows * top // (2 * experts))
    toks = n_dp * tok_rows
    slots_dp = n_dp * slots
    rows = experts * slots_dp
    quarter = hidden // n_dp
    chunk = GROUP * slots_dp
    both = 2 * width
    last = len(CHUNKS)
    dma = pltpu.SemaphoreType.DMA
    vmem = pltpu.VMEM
    anywhere = pl.BlockSpec(memory_space=pl.ANY)
    inside = pl.BlockSpec(memory_space=pltpu.VMEM)
    return pl.pallas_call(
        moe_kernel,
        out_shape=(
            jax.ShapeDtypeStruct(tokens.shape, BF),
            jax.ShapeDtypeStruct(tokens.shape, BF),
            jax.ShapeDtypeStruct((top, tok_rows), F32),
            jax.ShapeDtypeStruct((width, hidden), BF),
            jax.ShapeDtypeStruct((width, hidden), BF),
            jax.ShapeDtypeStruct((hidden, width), BF),
            jax.ShapeDtypeStruct((rows, both), BF),
            jax.ShapeDtypeStruct((experts * toks, both + LANES), BF),
        ),
        in_specs=[anywhere, anywhere, inside, inside, anywhere, anywhere, anywhere],
        out_specs=(anywhere, anywhere, inside) + (anywhere,) * 5,
        scratch_shapes=[
            vmem((width, hidden), BF),
            vmem((width, hidden), BF),
            vmem((hidden, width), BF),
            vmem((LANES, LANES), F32),
            vmem((tok_rows, LANES), BF),
            vmem((toks, both + LANES), BF),
            vmem((GROUP * toks, both + LANES), BF),
            vmem((chunk, width), BF),
            vmem((width, rows), BF),
            vmem((rows, width), BF),
            vmem((hidden, rows), BF),
            vmem((n_dp - 1, 3, rows, quarter), BF),
            vmem((3, rows, quarter), F32),
            vmem((2, 3, rows // 2, quarter), BF),
            vmem((2, 3, rows, quarter), BF),
            vmem((3, rows, hidden), BF),
            vmem((rows, both), BF),
            vmem((2, width, quarter), BF),
            vmem((2, quarter, width), BF),
            vmem((chunk, both), BF),
            vmem((toks, width), F32),
            vmem((toks, width), F32),
            vmem((toks, LANES), F32),
            vmem((toks, both), BF),
            vmem((n_dp, tok_rows, LANES), F32),
            dma((last, 2, 6)),
            dma((last, 2, 6)),
            dma((experts,)),
            dma((experts,)),
            dma((n_dp - 1, 3)),
            dma((n_dp - 1, 3)),
            dma((SIDE * SIDE, 4, 2)),
            dma((SIDE * SIDE, 2)),
            dma((SIDE * SIDE,)),
            dma((SIDE * SIDE,)),
            dma((10,)),
            dma((3, 2)),
            dma((n_dp, 3)),
            dma((n_dp - 1, 3)),
        ],
        compiler_params=pltpu.CompilerParams(
            collective_id=0, has_side_effects=True, vmem_limit_bytes=67043328
        ),
    )(tokens, out_grad, ids.T, weights.T, gate, up, down)


def per_device(tokens, ids, weights, out_grad, gate_weight, up_weight, down_weight):
    experts = lax.axis_size("expert")
    n_dp = lax.axis_size("dp")
    mixed, tgrad, route, gate_grad, up_grad, down_grad, _, _ = moe(
        tokens, out_grad, ids, weights, gate_weight[0], up_weight[0], down_weight[0], experts, n_dp
    )
    return (mixed, tgrad, route.T, gate_grad[None], up_grad[None], down_grad[None])


def solution(mesh):
    rows = P(("dp", "expert"), None)
    weights = (P("expert", "dp", None), P("expert", "dp", None), P("expert", None, "dp"))
    return jax.shard_map(
        per_device,
        mesh=mesh,
        in_specs=(rows, rows, rows, rows) + weights,
        out_specs=(rows, rows, rows) + weights,
        check_vma=False,
    )
```
